32 devices in a mesh: tm: 16 (over z, y, x), space: 2 (over core).
Axes of the slice: x: 2, y: 2, z: 4, core: 2. Of those that a mesh axis runs over, the one named last changes fastest.
Arguments:
- queries: bfloat16 [16, 8, 64, 1536], P('tm', 'space'), may hold values from -16 to 16
- keys: bfloat16 [16, 8, 64, 1536], P('tm', 'space'), may hold values from -16 to 16
- values: bfloat16 [16, 8, 64, 1536], P('tm', 'space'), may hold values from -6 to 6
- key_lists: int32 [16, 4, 6, 2], P('tm', 'space'), may hold values from 0 to 1, each once within a row
- density: int32 [16, 3], P('tm'), may hold values from 1 to 2
Outputs:
- attended: bfloat16 [16, 8, 64, 1536], P('tm', 'space')
The draws below stay inside these ranges and needn't reach their ends.
Inputs may be any that keep to these rules, and one draw needn't show every extreme that they name: `key_lists`: each list holds every block number of the partner band once.
All inputs are finite; a program needn't handle non-finite values.
Results may differ from the reference program's by a relative error of at most 0.0035.
Values may be sent and summed in bfloat16 or wider, within the bound.
No kernel may reach another device: no remote copies, remote signals or barrier semaphores. Data moves between devices by JAX's collectives and lax.ppermute only.
A program may use at most 64 MiB of HBM per device.

```python
import jax
import jax.numpy as jnp
from jax import lax

HEADS = 12
HEAD_DIM = 128
FW = 64
ROWS_DEV = 4
BROWS = 2
OFFSETS = 3
FRAMES = 16
HT = 8
HD = 1536
KB_DEV = 2
BLOCKS_FRAME = 4
SLOTS = 6
N_SPACE = 2


def drawn_pair(key):
    base_key = jax.random.fold_in(key, 4099)
    query_key, key_key = jax.random.split(base_key, 2)
    features = HEADS * HEAD_DIM
    shape = (FRAMES, HT, FW, features)
    query_out = jnp.clip(2.0 * jax.random.normal(query_key, shape, jnp.float32), -8.0, 8.0)
    key_out = jnp.clip(jax.random.normal(key_key, shape, jnp.float32), -6.0, 6.0)
    return (query_out, key_out)


def draw_queries(key, part):
    return drawn_pair(key)[0].astype(jnp.bfloat16)


def draw_keys(key, part):
    return drawn_pair(key)[1].astype(jnp.bfloat16)


def touch_ends(values, rng, low, top_value):
    longest = values.shape.index(max(values.shape))
    spots = []
    for shift in (0, 1):
        where = [jax.random.randint(jax.random.fold_in(rng, axis), (), 0, length) for axis, length in enumerate(values.shape)]
        where[longest] = (where[longest] + shift) % values.shape[longest]
        spots.append(tuple(where))
    return values.at[spots[0]].set(low).at[spots[1]].set(top_value)


def steps_of(own_key, shape, pieces, least, high):
    level, own = 1.0, jax.random.fold_in(own_key, 6)
    for position, blocks in pieces:
        draws = jnp.exp(jax.random.uniform(jax.random.fold_in(own, position), (blocks,), jnp.float32, least / len(pieces), high / len(pieces)))
        level = level * jnp.repeat(draws, shape[position] // blocks).reshape([-1 if axis == position else 1 for axis in range(len(shape))])
    return level


def gaussian(key, extent, deviation, limit, cuts=(), kind=jnp.bfloat16):
    values = jax.random.normal(key, extent, jnp.float32) * deviation
    if len(cuts) > 0:
        values = steps_of(key, extent, cuts, -0.22, 0.18) * values
    return jnp.clip(values, min=-limit, max=limit).astype(kind)


def setup_inputs(seed: int = 0) -> dict:
    seeds = jax.random.split(jax.random.key(seed), 6)
    return {
        "queries": draw_queries(jax.random.fold_in(seeds[5], 71), 0),
        "keys": draw_keys(jax.random.fold_in(seeds[5], 71), 0),
        "values": gaussian(seeds[2], (FRAMES, HT, FW, HD), 1.0, 6.0, ((0, 16), (1, 2))),
        "key_lists": jax.vmap(lambda own: jax.random.permutation(own, KB_DEV))(jax.random.split(seeds[3], FRAMES * BLOCKS_FRAME * SLOTS)).reshape((FRAMES, BLOCKS_FRAME, SLOTS, KB_DEV)).astype(jnp.int32),
        "density": touch_ends(jax.random.randint(seeds[4], (FRAMES, OFFSETS), 1, KB_DEV + 1), jax.random.fold_in(seeds[4], 1), 1, KB_DEV).astype(jnp.int32),
    }


def block_allowed(block_lists, live_counts):
    kb_count = block_lists.shape[2]
    positions = jnp.arange(kb_count, dtype=jnp.int32)
    live_cols = positions[None, :] < jnp.repeat(live_counts, 2)[:, None]
    matches = (block_lists[:, :, :, None] == positions[None, None, None, :]) & live_cols[None, :, :, None]
    return jnp.any(matches, axis=2)


def expand_blocks(allowed, block_tokens):
    q_count, slot_count, k_count = allowed.shape
    widened = jnp.broadcast_to(allowed[:, None, :, :, None], (q_count, block_tokens, slot_count, k_count, block_tokens))
    return widened.reshape(q_count * block_tokens, slot_count, k_count * block_tokens)


def attend(query_rows, key_rows, value_rows, mask):
    scale = 1.0 / float(HEAD_DIM) ** 0.5

    def one_head(head):
        query_head = lax.dynamic_slice_in_dim(query_rows, head * HEAD_DIM, HEAD_DIM, 1)
        key_head = lax.dynamic_slice_in_dim(key_rows, head * HEAD_DIM, HEAD_DIM, 1)
        value_head = lax.dynamic_slice_in_dim(value_rows, head * HEAD_DIM, HEAD_DIM, 1)
        scores = lax.dot_general(query_head, key_head, (((1,), (1,)), ((), ())), preferred_element_type=jnp.float32) * scale
        masked = jnp.where(mask, scores, -1e30)
        row_top = jnp.max(masked, axis=1, keepdims=True)
        weights = jnp.where(mask, jnp.exp(masked - row_top), 0.0)
        total = jnp.sum(weights, axis=1, keepdims=True)
        mixed = jnp.dot(weights.astype(jnp.bfloat16), value_head, preferred_element_type=jnp.float32) / total
        return mixed.astype(jnp.bfloat16)

    per_head = lax.map(one_head, jnp.arange(HEADS, dtype=jnp.int32))
    return jnp.transpose(per_head, (1, 0, 2)).reshape(query_rows.shape[0], HEADS * HEAD_DIM)


def reference(queries, keys, values, key_lists, density):
    features = HEADS * HEAD_DIM
    reach_frames = 2 ** (OFFSETS - 1)
    pad_widths = ((reach_frames, reach_frames), (BROWS, BROWS), (0, 0), (0, 0))
    padded_keys = jnp.pad(keys, pad_widths)
    padded_values = jnp.pad(values, pad_widths)
    tok_rows = ROWS_DEV * FW
    block_tokens = BROWS * FW
    kb_count = ROWS_DEV // BROWS
    row_ids = jnp.arange(ROWS_DEV + 2 * BROWS, dtype=jnp.int32)

    def group(group_index):
        frame_index = group_index // N_SPACE
        band_index = group_index % N_SPACE
        first_row = band_index * ROWS_DEV
        zero_index = jnp.int32(0)
        query_rows = lax.dynamic_slice(queries, (frame_index, first_row, zero_index, zero_index), (1, ROWS_DEV, FW, features)).reshape(tok_rows, features)
        near_shape = (1, ROWS_DEV + 2 * BROWS, FW, features)
        key_parts = [lax.dynamic_slice(padded_keys, (frame_index + reach_frames, first_row, zero_index, zero_index), near_shape).reshape(-1, features)]
        value_parts = [lax.dynamic_slice(padded_values, (frame_index + reach_frames, first_row, zero_index, zero_index), near_shape).reshape(-1, features)]
        global_rows = first_row - BROWS + row_ids
        row_ok = (global_rows >= 0) & (global_rows < HT)
        near_ok = jnp.repeat(row_ok, FW)
        slot_ok = []
        band_shape = (1, ROWS_DEV, FW, features)
        for degree in range(OFFSETS):
            for direction in (-1, 1):
                partner = frame_index + direction * 2 ** degree
                start = (partner + reach_frames, first_row + BROWS, zero_index, zero_index)
                key_parts.append(lax.dynamic_slice(padded_keys, start, band_shape).reshape(tok_rows, features))
                value_parts.append(lax.dynamic_slice(padded_values, start, band_shape).reshape(tok_rows, features))
                slot_ok.append((partner >= 0) & (partner < FRAMES))
        block_lists = lax.dynamic_slice(key_lists, (frame_index, band_index * kb_count, zero_index, zero_index), (1, kb_count, 2 * OFFSETS, kb_count))[0]
        live_counts = lax.dynamic_slice(density, (frame_index, zero_index), (1, OFFSETS))[0]
        allowed = expand_blocks(block_allowed(block_lists, live_counts), block_tokens)
        allowed = allowed & jnp.stack(slot_ok)[None, :, None]
        mask = jnp.concatenate([jnp.broadcast_to(near_ok[None, :], (tok_rows, near_ok.shape[0])), allowed.reshape(tok_rows, -1)], axis=1)
        return attend(query_rows, jnp.concatenate(key_parts, axis=0), jnp.concatenate(value_parts, axis=0), mask)

    result = lax.map(group, jnp.arange(FRAMES * N_SPACE, dtype=jnp.int32))
    return result.reshape(FRAMES, N_SPACE, ROWS_DEV, FW, features).reshape(FRAMES, HT, FW, features)
```

```python
import math

import jax
import jax.numpy as jnp
from jax import lax
from jax.experimental import pallas as pl
from jax.experimental.pallas import tpu as pltpu
from jax.sharding import PartitionSpec as P


HEADS = 12
HEAD_DIM = 128
BROWS = 2
OFFSETS = 3
GROUP = 2 ** (OFFSETS - 1)
HEADS_STEP = 3
NEG = -1e30
SCALE2 = math.log2(math.e) / math.sqrt(HEAD_DIM)


def routes(count):
    def pairs(target):
        out = []
        for t in range(count):
            to = target(t, t % GROUP)
            if to is not None and 0 <= to < count:
                out.append((t, to))
        return out

    up = GROUP // 2
    return {
        "x": pairs(lambda t, p: t ^ 1),
        "y": pairs(lambda t, p: t ^ 2),
        "o": pairs(lambda t, p: t - GROUP if p < up else t + GROUP),
        "b": pairs(lambda t, p: t + GROUP if p < up else t - GROUP),
        "g": pairs(lambda t, p: t ^ 1 if p in (0, GROUP - 1) else None),
        "e": pairs(lambda t, p: t ^ 1 if p not in (0, GROUP - 1) else None),
    }


def slot_of(name, p):
    low = (p < GROUP // 2).astype(jnp.int32)
    even = 1 - p % 2
    return {
        "X": even,
        "Y": 2 + low,
        "O": 4 + low,
        "B": 5 - low,
        "W": 3 - low,
        "GE": 1 - even,
    }[name]


def dot_nt(a, b):
    return lax.dot_general(a, b, (((1,), (1,)), ((), ())), preferred_element_type=jnp.float32)


def flash(q, blocks, state, halves):
    rows = q.shape[0] // halves
    scores = [dot_nt(q, k) for k, _, _ in blocks]
    tops = []
    for half in range(halves):
        top = None
        for s, (_, _, allow) in zip(scores, blocks):
            part = s[half * rows : (half + 1) * rows]
            width = part.shape[1] // len(allow[half])
            for kb, ok in enumerate(allow[half]):
                piece = part[:, kb * width : (kb + 1) * width]
                if ok is not None:
                    piece = jnp.where(ok, piece, NEG)
                for lane in range(0, width, 128):
                    lanes = piece[:, lane : lane + 128]
                    top = lanes if top is None else jnp.maximum(top, lanes)
        tops.append(jnp.max(top, axis=1, keepdims=True))
    top = jnp.concatenate(tops, axis=0)
    if state is not None:
        old_top, old_total, old_acc = state
        top = jnp.maximum(top, old_top)
    shift = top * SCALE2
    lane_sum = None
    acc = None
    for s, (_, v, allow) in zip(scores, blocks):
        rows_out = []
        for half in range(halves):
            part = s[half * rows : (half + 1) * rows]
            own = shift[half * rows : (half + 1) * rows]
            width = part.shape[1] // len(allow[half])
            cols = []
            for kb, ok in enumerate(allow[half]):
                off = own if ok is None else jnp.where(ok, own, -NEG)
                cols.append(jnp.exp2(part[:, kb * width : (kb + 1) * width] * SCALE2 - off))
            rows_out.append(cols[0] if len(cols) == 1 else jnp.concatenate(cols, axis=1))
        w = jnp.concatenate(rows_out, axis=0)
        for lane in range(0, w.shape[1], 128):
            lanes = w[:, lane : lane + 128]
            lane_sum = lanes if lane_sum is None else lane_sum + lanes
        mixed = jnp.dot(w.astype(jnp.bfloat16), v, preferred_element_type=jnp.float32)
        acc = mixed if acc is None else acc + mixed
    total = jnp.sum(lane_sum, axis=1, keepdims=True)
    if state is not None:
        decay = jnp.exp2((old_top - top) * SCALE2)
        total = total + old_total * decay
        acc = acc + old_acc * decay
    return top, total, acc


def stage_call(q, entries, state, lists, density, final):
    tokens, features = q.shape
    width = HEADS_STEP * HEAD_DIM
    steps = features // width
    kinds = [kind for kind, _, _ in entries]
    halves = lists.shape[1]
    positions = lists.shape[3]
    frames = lax.axis_size("tm")
    bands = lax.axis_size("space")
    n_in = 2 * len(entries)

    def kernel(lists_ref, density_ref, *refs):
        q_ref = refs[0]
        kv = refs[1 : 1 + n_in]
        rest = refs[1 + n_in :]
        if state is not None:
            stat_in, acc_in = rest[:2]
            rest = rest[2:]
        t = lax.axis_index("tm")
        band = lax.axis_index("space")
        p = t % GROUP

        def allow_of(kind):
            if kind == "own":
                return [[None]] * halves
            if kind == "before":
                return [[band > 0]] * halves
            if kind == "after":
                return [[band < bands - 1]] * halves
            slot = slot_of(kind, p)
            step = jnp.left_shift(1, slot // 2)
            there = t + jnp.where(slot % 2 == 0, -step, step)
            ok = (there >= 0) & (there < frames)
            live = density_ref[0, slot // 2]
            out = []
            for half in range(halves):
                row = []
                for kb in range(positions):
                    hit = (lists_ref[0, half, slot, 0] == kb) & (live > 0)
                    for i in range(1, positions):
                        hit = hit | ((lists_ref[0, half, slot, i] == kb) & (live > i))
                    row.append(ok & hit)
                out.append(row)
            return out

        allows = [allow_of(kind) for kind in kinds if kind != "E"]
        wrap = (p == 0) | (p == GROUP - 1)
        for h in range(HEADS_STEP):
            cols = slice(h * HEAD_DIM, (h + 1) * HEAD_DIM)
            blocks = []
            for i, kind in enumerate(kinds):
                if kind == "E":
                    continue
                k, v = kv[2 * i][:, cols], kv[2 * i + 1][:, cols]
                if kind == "GE":
                    j = kinds.index("E")
                    k = jnp.where(wrap, kv[2 * j][:, cols], k)
                    v = jnp.where(wrap, kv[2 * j + 1][:, cols], v)
                blocks.append((k, v, allows[len(blocks)]))
            old = None
            if state is not None:
                stat = stat_in[:, cols]
                old = (stat[:, 0:1], stat[:, HEAD_DIM // 2 : HEAD_DIM // 2 + 1], acc_in[:, cols])
            top, total, acc = flash(q_ref[:, cols], blocks, old, halves)
            if final:
                rest[0][:, cols] = (acc / total).astype(jnp.bfloat16)
            else:
                lane = lax.broadcasted_iota(jnp.int32, (tokens, HEAD_DIM), 1)
                rest[0][:, cols] = jnp.where(lane < HEAD_DIM // 2, top, total)
                rest[1][:, cols] = acc

    def spec(rows):
        return pl.BlockSpec((rows, width), lambda i: (0, i))

    smem = pl.BlockSpec(memory_space=pltpu.SMEM)
    operands = [lists, density, q]
    specs = [smem, smem, spec(tokens)]
    keys = 0
    for kind, k, v in entries:
        operands += [k, v]
        specs += [spec(k.shape[0]), spec(v.shape[0])]
        keys += k.shape[0] if kind != "E" else 0
    if state is not None:
        operands += list(state)
        specs += [spec(tokens), spec(tokens)]
    full = jax.ShapeDtypeStruct((tokens, features), jnp.float32)
    if final:
        outs, out_specs = jax.ShapeDtypeStruct((tokens, features), jnp.bfloat16), spec(tokens)
    else:
        outs, out_specs = (full, full), (spec(tokens), spec(tokens))
    return pl.pallas_call(
        kernel,
        grid=(steps,),
        in_specs=specs,
        out_specs=out_specs,
        out_shape=outs,
        cost_estimate=pl.CostEstimate(
            flops=4 * tokens * keys * features,
            transcendentals=tokens * keys * HEADS,
            bytes_accessed=2 * features * (2 * keys + 4 * tokens),
        ),
    )(*operands)


def body(queries, keys, values, key_lists, density):
    _, rows_dev, width, features = queries.shape
    frames = lax.axis_size("tm")
    bands = lax.axis_size("space")
    route = routes(frames)
    up = [(i, i + 1) for i in range(bands - 1)]
    down = [(j, i) for i, j in up]

    def send(value, pairs, axis="tm"):
        return lax.ppermute(value, axis, pairs)

    def flat(value):
        return value.reshape(-1, features)

    edge = BROWS
    y_k = send(keys, route["y"])
    x_k = send(keys, route["x"])
    o_k = send(keys, route["o"])
    b_k = send(keys, route["b"])
    last = jnp.concatenate([keys[:, rows_dev - edge :], values[:, rows_dev - edge :]], axis=0)
    first = jnp.concatenate([keys[:, :edge], values[:, :edge]], axis=0)
    before = send(last, up, "space")
    after = send(first, down, "space")
    y_v = send(values, route["y"])
    x_v = send(values, route["x"])
    o_v = send(values, route["o"])
    w_k = send(y_k, route["b"])
    g_k = send(y_k, route["g"])
    w_v = send(y_v, route["b"])
    e_k = send(w_k, route["e"])
    g_v = send(y_v, route["g"])
    b_v = send(values, route["b"])
    e_v = send(w_v, route["e"])

    q = flat(queries)
    state = stage_call(
        q,
        [
            ("own", flat(keys), flat(values)),
            ("before", flat(before[0]), flat(before[1])),
            ("after", flat(after[0]), flat(after[1])),
        ],
        None,
        key_lists,
        density,
        False,
    )
    state = stage_call(
        q,
        [("X", flat(x_k), flat(x_v)), ("Y", flat(y_k), flat(y_v)), ("O", flat(o_k), flat(o_v))],
        state,
        key_lists,
        density,
        False,
    )
    state = stage_call(q, [("W", flat(w_k), flat(w_v))], state, key_lists, density, False)
    result = stage_call(
        q,
        [("B", flat(b_k), flat(b_v)), ("GE", flat(g_k), flat(g_v)), ("E", flat(e_k), flat(e_v))],
        state,
        key_lists,
        density,
        True,
    )
    return result.reshape(1, rows_dev, width, features)


def solution(mesh):
    in_specs = (
        P("tm", "space", None, None),
        P("tm", "space", None, None),
        P("tm", "space", None, None),
        P("tm", "space", None, None),
        P("tm", None),
    )
    out_specs = P("tm", "space", None, None)
    return jax.shard_map(body, mesh=mesh, in_specs=in_specs, out_specs=out_specs, check_vma=False)
```

```python
import math

import jax
import jax.numpy as jnp
from jax import lax
from jax.experimental import pallas as pl
from jax.experimental.pallas import tpu as pltpu
from jax.sharding import PartitionSpec as P


HEAD_DIM = 128
OFFSETS = 3
GROUP = 2 ** (OFFSETS - 1)
SUBLANES = 8
UNROLL = 4
VMEM_LIMIT = 16 * 2**20
NEG = -1e30
SCALE2 = math.log2(math.e) / math.sqrt(HEAD_DIM)


def routes(count):
    def pairs(target):
        out = []
        for t in range(count):
            to = target(t, t % GROUP)
            if to is not None and 0 <= to < count:
                out.append((t, to))
        return out

    up = GROUP // 2
    return {
        "x": pairs(lambda t, p: t ^ 1),
        "y": pairs(lambda t, p: t ^ 2),
        "o": pairs(lambda t, p: t - GROUP if p < up else t + GROUP),
        "b": pairs(lambda t, p: t + GROUP if p < up else t - GROUP),
        "g": pairs(lambda t, p: t ^ 1 if p in (0, GROUP - 1) else None),
        "e": pairs(lambda t, p: t ^ 1 if p not in (0, GROUP - 1) else None),
    }


def slot_of(name, p):
    low = (p < GROUP // 2).astype(jnp.int32)
    even = 1 - p % 2
    return {
        "X": even,
        "Y": 2 + low,
        "O": 4 + low,
        "B": 5 - low,
        "W": 3 - low,
        "GE": 1 - even,
    }[name]


def contract(a, b, dims):
    return lax.dot_general(a, b, (dims, ((), ())), preferred_element_type=jnp.float32)


def fold(value, op):
    return op(value.reshape(-1, SUBLANES, value.shape[1]), axis=0)


def flash(q, blocks, state, halves):
    lanes = q.shape[0] // halves
    scores = [contract(k, q, ((1,), (1,))) for k, _, _ in blocks]
    tops, shifts = [], []
    for half in range(halves):
        cols = slice(half * lanes, (half + 1) * lanes)
        top = None if state is None else state[0][:, cols]
        for s, (_, _, allow) in zip(scores, blocks):
            rows = s.shape[0] // len(allow[half])
            for kb, ok in enumerate(allow[half]):
                piece = fold(s[kb * rows : (kb + 1) * rows, cols], jnp.max)
                if ok is not None:
                    piece = jnp.where(ok, piece, NEG)
                top = piece if top is None else jnp.maximum(top, piece)
        top = jnp.max(top, axis=0, keepdims=True)
        tops.append(top)
        shifts.append(top * SCALE2)
    sums = [None] * halves
    acc = None
    for s, (_, v, allow) in zip(scores, blocks):
        parts = []
        for half in range(halves):
            cols = slice(half * lanes, (half + 1) * lanes)
            rows = s.shape[0] // len(allow[half])
            down = []
            for kb, ok in enumerate(allow[half]):
                off = shifts[half] if ok is None else jnp.where(ok, shifts[half], -NEG)
                w = jnp.exp2(s[kb * rows : (kb + 1) * rows, cols] * SCALE2 - off)
                part = fold(w, jnp.sum)
                sums[half] = part if sums[half] is None else sums[half] + part
                down.append(w.astype(jnp.bfloat16))
            parts.append(down[0] if len(down) == 1 else jnp.concatenate(down, axis=0))
        mixed = contract(v, jnp.concatenate(parts, axis=1), ((0,), (0,)))
        acc = mixed if acc is None else acc + mixed
    top = jnp.concatenate(tops, axis=1)
    total = jnp.concatenate(sums, axis=1)
    if state is not None:
        decay = jnp.exp2((state[0][0:1] - top) * SCALE2)
        total = total + state[1] * decay
        acc = acc + state[2] * decay
    return top, total, acc


def stage_call(q, entries, state, lists, density, final):
    tokens, features = q.shape
    heads = features // HEAD_DIM
    kinds = [kind for kind, _, _ in entries]
    halves = lists.shape[1]
    positions = lists.shape[3]
    frames = lax.axis_size("tm")
    bands = lax.axis_size("space")
    edge = tokens // halves
    n_in = 2 * len(entries)

    def kernel(lists_ref, density_ref, *refs):
        q_ref = refs[0]
        kv = refs[1 : 1 + n_in]
        rest = refs[1 + n_in :]
        old_refs = None
        if state is not None:
            old_refs = rest[:3]
            rest = rest[3:]
        t = lax.axis_index("tm")
        band = lax.axis_index("space")
        p = t % GROUP

        def allow_of(kind):
            if kind in ("own", "other"):
                return [[None]] * halves
            if kind == "before":
                return [[band > 0]] * halves
            if kind == "after":
                return [[band < bands - 1]] * halves
            slot = slot_of(kind, p)
            step = jnp.left_shift(1, slot // 2)
            there = t + jnp.where(slot % 2 == 0, -step, step)
            ok = (there >= 0) & (there < frames)
            live = density_ref[0, slot // 2]
            out = []
            for half in range(halves):
                row = []
                for kb in range(positions):
                    hit = (lists_ref[0, half, slot, 0] == kb) & (live > 0)
                    for i in range(1, positions):
                        hit = hit | ((lists_ref[0, half, slot, i] == kb) & (live > i))
                    row.append(ok & hit)
                out.append(row)
            return out

        rows_of = {
            "before": pl.ds(tokens - edge, edge),
            "after": pl.ds(0, edge),
            "other": pl.ds(pl.multiple_of(jnp.where(band > 0, tokens - edge, 0), edge), edge),
        }
        allows = [allow_of(kind) for kind in kinds if kind != "E"]
        wrap = (p == 0) | (p == GROUP - 1)

        def one_head(h, carry):
            cols = pl.ds(pl.multiple_of(h * HEAD_DIM, HEAD_DIM), HEAD_DIM)
            blocks = []
            for i, kind in enumerate(kinds):
                if kind == "E":
                    continue
                rows = rows_of.get(kind, slice(None))
                k, v = kv[2 * i][rows, cols], kv[2 * i + 1][rows, cols]
                if kind == "GE":
                    j = kinds.index("E")
                    k = jnp.where(wrap, kv[2 * j][:, cols], k)
                    v = jnp.where(wrap, kv[2 * j + 1][:, cols], v)
                blocks.append((k, v, allows[len(blocks)]))
            old = None if state is None else [ref[h] for ref in old_refs]
            top, total, acc = flash(q_ref[:, cols], blocks, old, halves)
            if final:
                scaled = acc * (1.0 / jnp.sum(total, axis=0, keepdims=True))
                rest[0][:, cols] = jnp.transpose(scaled).astype(jnp.bfloat16)
            else:
                rest[0][h] = jnp.broadcast_to(top, (SUBLANES, tokens))
                rest[1][h] = total
                rest[2][h] = acc
            return carry

        lax.fori_loop(0, heads, one_head, 0, unroll=UNROLL)

    smem = pl.BlockSpec(memory_space=pltpu.SMEM)
    vmem = pl.BlockSpec(memory_space=pltpu.VMEM)
    operands = [lists, density, q]
    keys = 0
    for kind, k, v in entries:
        operands += [k, v]
        keys += k.shape[0] if kind != "E" else 0
    if state is not None:
        operands += list(state)
    operands = operands[:2] + [
        pltpu.with_memory_space_constraint(value, pltpu.VMEM) for value in operands[2:]
    ]
    specs = [smem, smem] + [vmem] * (len(operands) - 2)
    if final:
        outs, out_specs = jax.ShapeDtypeStruct((tokens, features), jnp.bfloat16), vmem
    else:
        small = pltpu.VMEM((heads, SUBLANES, tokens), jnp.float32)
        large = pltpu.VMEM((heads, HEAD_DIM, tokens), jnp.float32)
        outs, out_specs = (small, small, large), (vmem, vmem, vmem)
    return pl.pallas_call(
        kernel,
        in_specs=specs,
        out_specs=out_specs,
        out_shape=outs,
        compiler_params=pltpu.CompilerParams(vmem_limit_bytes=VMEM_LIMIT),
        cost_estimate=pl.CostEstimate(
            flops=4 * tokens * keys * features,
            transcendentals=tokens * keys * heads,
            bytes_accessed=2 * features * (2 * keys + 4 * tokens),
        ),
    )(*operands)


def body(queries, keys, values, key_lists, density):
    _, rows_dev, width, features = queries.shape
    frames = lax.axis_size("tm")
    bands = lax.axis_size("space")
    route = routes(frames)
    up = [(i, i + 1) for i in range(bands - 1)]
    down = [(j, i) for i, j in up]

    def send(value, pairs, axis="tm"):
        return lax.ppermute(value, axis, pairs)

    def flat(value):
        return value.reshape(-1, features)

    y_k = send(keys, route["y"])
    x_k = send(keys, route["x"])
    o_k = send(keys, route["o"])
    b_k = send(keys, route["b"])
    y_v = send(values, route["y"])
    x_v = send(values, route["x"])
    o_v = send(values, route["o"])
    if bands == 2:
        s_k = send(keys, up + down, "space")
        s_v = send(values, up + down, "space")
        beside = [("other", flat(s_k), flat(s_v))]
    else:
        up_k = send(keys, up, "space")
        up_v = send(values, up, "space")
        down_k = send(keys, down, "space")
        down_v = send(values, down, "space")
        beside = [("before", flat(up_k), flat(up_v)), ("after", flat(down_k), flat(down_v))]
    w_k = send(y_k, route["b"])
    g_k = send(y_k, route["g"])
    w_v = send(y_v, route["b"])
    e_k = send(w_k, route["e"])
    g_v = send(y_v, route["g"])
    b_v = send(values, route["b"])
    e_v = send(w_v, route["e"])

    q = flat(queries)
    state = stage_call(
        q, [("own", flat(keys), flat(values))] + beside, None, key_lists, density, False
    )
    state = stage_call(
        q,
        [
            ("X", flat(x_k), flat(x_v)),
            ("Y", flat(y_k), flat(y_v)),
            ("O", flat(o_k), flat(o_v)),
        ],
        state,
        key_lists,
        density,
        False,
    )
    state = stage_call(
        q, [("W", flat(w_k), flat(w_v))], state, key_lists, density, False
    )
    result = stage_call(
        q,
        [
            ("B", flat(b_k), flat(b_v)),
            ("GE", flat(g_k), flat(g_v)),
            ("E", flat(e_k), flat(e_v)),
        ],
        state,
        key_lists,
        density,
        True,
    )
    return result.reshape(1, rows_dev, width, features)


def solution(mesh):
    in_specs = (
        P("tm", "space", None, None),
        P("tm", "space", None, None),
        P("tm", "space", None, None),
        P("tm", "space", None, None),
        P("tm", None),
    )
    out_specs = P("tm", "space", None, None)
    return jax.shard_map(body, mesh=mesh, in_specs=in_specs, out_specs=out_specs, check_vma=False)
```

```python
import math

import jax
import jax.numpy as jnp
from jax import lax
from jax.experimental import pallas as pl
from jax.experimental.pallas import tpu as pltpu
from jax.sharding import PartitionSpec as P


HEAD_DIM = 128
OFFSETS = 3
GROUP = 2 ** (OFFSETS - 1)
SUBLANES = 8
UNROLL = 4
VMEM_LIMIT = 16 * 2**20
NEG = -1e30
SCALE2 = math.log2(math.e) / math.sqrt(HEAD_DIM)


def routes(count):
    def pairs(target):
        out = []
        for t in range(count):
            to = target(t, t % GROUP)
            if to is not None and 0 <= to < count:
                out.append((t, to))
        return out

    up = GROUP // 2
    return {
        "x": pairs(lambda t, p: t ^ 1),
        "y": pairs(lambda t, p: t ^ 2),
        "o": pairs(lambda t, p: t - GROUP if p < up else t + GROUP),
        "b": pairs(lambda t, p: t + GROUP if p < up else t - GROUP),
        "in_x": pairs(lambda t, p: t ^ 1 if p in (0, GROUP - 1) else None),
        "in_y": pairs(lambda t, p: t ^ 2 if p in (0, GROUP - 1) else None),
        "out_x": pairs(lambda t, p: t ^ 1 if p not in (0, GROUP - 1) else None),
        "out_y": pairs(lambda t, p: t ^ 2 if p not in (0, GROUP - 1) else None),
    }


def slot_of(name, p):
    low = (p < GROUP // 2).astype(jnp.int32)
    even = 1 - p % 2
    return {
        "X": even,
        "Y": 2 + low,
        "O": 4 + low,
        "B": 5 - low,
        "W": 3 - low,
        "GE": 1 - even,
    }[name]


def contract(a, b, dims):
    return lax.dot_general(a, b, (dims, ((), ())), preferred_element_type=jnp.float32)


def fold(value, op):
    return op(value.reshape(-1, SUBLANES, value.shape[1]), axis=0)


def flash(q, blocks, state, halves):
    lanes = q.shape[0] // halves
    scores = [contract(k, q, ((1,), (1,))) for k, _, _ in blocks]
    tops, shifts = [], []
    for half in range(halves):
        cols = slice(half * lanes, (half + 1) * lanes)
        top = None if state is None else state[0][:, cols]
        for s, (_, _, allow) in zip(scores, blocks):
            rows = s.shape[0] // len(allow[half])
            for kb, ok in enumerate(allow[half]):
                piece = fold(s[kb * rows : (kb + 1) * rows, cols], jnp.max)
                if ok is not None:
                    piece = jnp.where(ok, piece, NEG)
                top = piece if top is None else jnp.maximum(top, piece)
        top = jnp.max(top, axis=0, keepdims=True)
        tops.append(top)
        shifts.append(top * SCALE2)
    sums = [None] * halves
    acc = None
    for s, (_, v, allow) in zip(scores, blocks):
        parts = []
        for half in range(halves):
            cols = slice(half * lanes, (half + 1) * lanes)
            rows = s.shape[0] // len(allow[half])
            down = []
            for kb, ok in enumerate(allow[half]):
                off = shifts[half] if ok is None else jnp.where(ok, shifts[half], -NEG)
                w = jnp.exp2(s[kb * rows : (kb + 1) * rows, cols] * SCALE2 - off)
                part = fold(w, jnp.sum)
                sums[half] = part if sums[half] is None else sums[half] + part
                down.append(w.astype(jnp.bfloat16))
            parts.append(down[0] if len(down) == 1 else jnp.concatenate(down, axis=0))
        mixed = contract(v, jnp.concatenate(parts, axis=1), ((0,), (0,)))
        acc = mixed if acc is None else acc + mixed
    top = jnp.concatenate(tops, axis=1)
    total = jnp.concatenate(sums, axis=1)
    if state is not None:
        decay = jnp.exp2((state[0][0:1] - top) * SCALE2)
        total = total + state[1] * decay
        acc = acc + state[2] * decay
    return top, total, acc


def stage_call(q, entries, state, lists, density, final):
    tokens, features = q.shape
    heads = features // HEAD_DIM
    kinds = [entry[0] for entry in entries]
    starts = [sum(len(e) - 1 for e in entries[:i]) for i in range(len(entries) + 1)]
    halves = lists.shape[1]
    positions = lists.shape[3]
    frames = lax.axis_size("tm")
    bands = lax.axis_size("space")
    edge = tokens // halves
    n_in = starts[-1]

    def kernel(lists_ref, density_ref, *refs):
        q_ref = refs[0]
        kv = refs[1 : 1 + n_in]
        rest = refs[1 + n_in :]
        old_refs = None
        if state is not None:
            old_refs = rest[:3]
            rest = rest[3:]
        t = lax.axis_index("tm")
        band = lax.axis_index("space")
        p = t % GROUP

        def allow_of(kind):
            if kind in ("own", "other"):
                return [[None]] * halves
            if kind == "before":
                return [[band > 0]] * halves
            if kind == "after":
                return [[band < bands - 1]] * halves
            slot = slot_of(kind, p)
            step = jnp.left_shift(1, slot // 2)
            there = t + jnp.where(slot % 2 == 0, -step, step)
            ok = (there >= 0) & (there < frames)
            live = density_ref[0, slot // 2]
            out = []
            for half in range(halves):
                row = []
                for kb in range(positions):
                    hit = (lists_ref[0, half, slot, 0] == kb) & (live > 0)
                    for i in range(1, positions):
                        hit = hit | ((lists_ref[0, half, slot, i] == kb) & (live > i))
                    row.append(ok & hit)
                out.append(row)
            return out

        rows_of = {
            "before": pl.ds(tokens - edge, edge),
            "after": pl.ds(0, edge),
            "other": pl.ds(pl.multiple_of(jnp.where(band > 0, tokens - edge, 0), edge), edge),
        }
        allows = [allow_of(kind) for kind in kinds if kind != "E"]
        wrap = (p == 0) | (p == GROUP - 1)

        def pair_of(i, rows, cols):
            k, *parts = [ref[rows, cols] for ref in kv[starts[i] : starts[i + 1]]]
            return k, parts[0] if len(parts) == 1 else jnp.concatenate(parts, axis=0)

        def one_head(h, carry):
            cols = pl.ds(pl.multiple_of(h * HEAD_DIM, HEAD_DIM), HEAD_DIM)
            blocks = []
            for i, kind in enumerate(kinds):
                if kind == "E":
                    continue
                rows = rows_of.get(kind, slice(None))
                k, v = pair_of(i, rows, cols)
                if kind == "GE":
                    wrap_k, wrap_v = pair_of(kinds.index("E"), rows, cols)
                    k = jnp.where(wrap, wrap_k, k)
                    v = jnp.where(wrap, wrap_v, v)
                blocks.append((k, v, allows[len(blocks)]))
            old = None if state is None else [ref[h] for ref in old_refs]
            top, total, acc = flash(q_ref[:, cols], blocks, old, halves)
            if final:
                scaled = acc * (1.0 / jnp.sum(total, axis=0, keepdims=True))
                rest[0][:, cols] = jnp.transpose(scaled).astype(jnp.bfloat16)
            else:
                rest[0][h] = jnp.broadcast_to(top, (SUBLANES, tokens))
                rest[1][h] = total
                rest[2][h] = acc
            return carry

        lax.fori_loop(0, heads, one_head, 0, unroll=UNROLL)

    smem = pl.BlockSpec(memory_space=pltpu.SMEM)
    vmem = pl.BlockSpec(memory_space=pltpu.VMEM)
    operands = [lists, density, q]
    keys = 0
    for kind, k, *v in entries:
        operands += [k, *v]
        keys += k.shape[0] if kind != "E" else 0
    if state is not None:
        operands += list(state)
    operands = operands[:2] + [
        pltpu.with_memory_space_constraint(value, pltpu.VMEM) for value in operands[2:]
    ]
    specs = [smem, smem] + [vmem] * (len(operands) - 2)
    if final:
        outs, out_specs = jax.ShapeDtypeStruct((tokens, features), jnp.bfloat16), vmem
    else:
        small = pltpu.VMEM((heads, SUBLANES, tokens), jnp.float32)
        large = pltpu.VMEM((heads, HEAD_DIM, tokens), jnp.float32)
        outs, out_specs = (small, small, large), (vmem, vmem, vmem)
    return pl.pallas_call(
        kernel,
        in_specs=specs,
        out_specs=out_specs,
        out_shape=outs,
        compiler_params=pltpu.CompilerParams(vmem_limit_bytes=VMEM_LIMIT),
        cost_estimate=pl.CostEstimate(
            flops=4 * tokens * keys * features,
            transcendentals=tokens * keys * heads,
            bytes_accessed=2 * features * (2 * keys + 4 * tokens),
        ),
    )(*operands)


def body(queries, keys, values, key_lists, density):
    _, rows_dev, width, features = queries.shape
    frames = lax.axis_size("tm")
    bands = lax.axis_size("space")
    route = routes(frames)
    up = [(i, i + 1) for i in range(bands - 1)]
    down = [(j, i) for i, j in up]

    def send(value, pairs, axis="tm"):
        return lax.ppermute(value, axis, pairs)

    def flat(value):
        return value.reshape(-1, features)

    half = rows_dev // 2
    values0, values1 = values[:, :half], values[:, half:]
    y_k = send(keys, route["y"])
    x_k = send(keys, route["x"])
    o_k = send(keys, route["o"])
    b_k = send(keys, route["b"])
    y_v1 = send(values1, route["y"])
    x_v = send(values, route["x"])
    o_v0 = send(values0, route["o"])
    y_v0 = send(values0, route["y"])
    o_v1 = send(values1, route["o"])
    if bands == 2:
        s_k = send(keys, up + down, "space")
        s_v = send(values, up + down, "space")
        beside = [("other", flat(s_k), flat(s_v))]
    else:
        up_k = send(keys, up, "space")
        up_v = send(values, up, "space")
        down_k = send(keys, down, "space")
        down_v = send(values, down, "space")
        beside = [("before", flat(up_k), flat(up_v)), ("after", flat(down_k), flat(down_v))]

    w_k = send(y_k, route["b"])
    g_k = send(y_k, route["in_x"])
    w_v1 = send(y_v1, route["b"])
    f_v0 = send(o_v0, route["in_x"])
    w_v0 = send(o_v0, route["y"])
    e_k = send(w_k, route["out_x"])
    g_v = send(x_v, route["in_y"])
    b_v = send(values, route["b"])
    e_v0 = send(f_v0, route["out_y"])
    e_v1 = send(w_v1, route["out_x"])

    q = flat(queries)
    state = stage_call(
        q, [("own", flat(keys), flat(values))] + beside, None, key_lists, density, False
    )
    state = stage_call(
        q,
        [
            ("X", flat(x_k), flat(x_v)),
            ("Y", flat(y_k), flat(y_v0), flat(y_v1)),
        ],
        state,
        key_lists,
        density,
        False,
    )
    state = stage_call(
        q,
        [
            ("O", flat(o_k), flat(o_v0), flat(o_v1)),
            ("W", flat(w_k), flat(w_v0), flat(w_v1)),
        ],
        state,
        key_lists,
        density,
        False,
    )
    result = stage_call(
        q,
        [
            ("B", flat(b_k), flat(b_v)),
            ("GE", flat(g_k), flat(g_v)),
            ("E", flat(e_k), flat(e_v0), flat(e_v1)),
        ],
        state,
        key_lists,
        density,
        True,
    )
    return result.reshape(1, rows_dev, width, features)


def solution(mesh):
    in_specs = (
        P("tm", "space", None, None),
        P("tm", "space", None, None),
        P("tm", "space", None, None),
        P("tm", "space", None, None),
        P("tm", None),
    )
    out_specs = P("tm", "space", None, None)
    return jax.shard_map(body, mesh=mesh, in_specs=in_specs, out_specs=out_specs, check_vma=False)
```

```python
import math

import jax
import jax.numpy as jnp
from jax import lax
from jax.experimental import pallas as pl
from jax.experimental.pallas import tpu as pltpu
from jax.sharding import PartitionSpec as P


HEAD_DIM = 128
OFFSETS = 3
GROUP = 2 ** (OFFSETS - 1)
SUBLANES = 8
UNROLL = 2
VMEM_LIMIT = 16 * 2**20
NEG = -1e30
SCALE2 = math.log2(math.e) / math.sqrt(HEAD_DIM)


def routes(count):
    def pairs(target):
        out = []
        for t in range(count):
            to = target(t, t % GROUP)
            if to is not None and 0 <= to < count:
                out.append((t, to))
        return out

    up = GROUP // 2
    return {
        "x": pairs(lambda t, p: t ^ 1),
        "y": pairs(lambda t, p: t ^ 2),
        "o": pairs(lambda t, p: t - GROUP if p < up else t + GROUP),
        "b": pairs(lambda t, p: t + GROUP if p < up else t - GROUP),
        "in_x": pairs(lambda t, p: t ^ 1 if p in (0, GROUP - 1) else None),
        "in_y": pairs(lambda t, p: t ^ 2 if p in (0, GROUP - 1) else None),
        "out_x": pairs(lambda t, p: t ^ 1 if p not in (0, GROUP - 1) else None),
        "out_y": pairs(lambda t, p: t ^ 2 if p not in (0, GROUP - 1) else None),
    }


def slot_of(name, p):
    low = (p < GROUP // 2).astype(jnp.int32)
    even = 1 - p % 2
    return {
        "X": even,
        "Y": 2 + low,
        "O": 4 + low,
        "B": 5 - low,
        "W": 3 - low,
        "GE": 1 - even,
    }[name]


def contract(a, b, dims):
    return lax.dot_general(a, b, (dims, ((), ())), preferred_element_type=jnp.float32)


def fold_max(value):
    return jnp.max(value.reshape(-1, SUBLANES, value.shape[1]), axis=0)


def join(parts, axis):
    return parts[0] if len(parts) == 1 else jnp.concatenate(parts, axis=axis)


def stage_call(q, entries, state, lists, density, final):
    tokens, features = q.shape
    heads = features // HEAD_DIM
    kinds = [entry[0] for entry in entries]
    starts = [0]
    for _, k, v in entries:
        starts += [starts[-1] + len(k), starts[-1] + len(k) + len(v)]
    halves = lists.shape[1]
    positions = lists.shape[3]
    frames = lax.axis_size("tm")
    bands = lax.axis_size("space")
    edge = tokens // halves
    n_in = starts[-1]

    def kernel(lists_ref, density_ref, *refs):
        q_ref = refs[0]
        kv = refs[1 : 1 + n_in]
        rest, scratch = refs[1 + n_in : -4], refs[-4:]
        old_refs = None
        if state is not None:
            old_refs = rest[:3]
            rest = rest[3:]
        t = lax.axis_index("tm")
        band = lax.axis_index("space")
        p = t % GROUP

        def allow_of(kind):
            if kind in ("own", "other"):
                return [[None]] * halves
            if kind == "before":
                return [[band > 0]] * halves
            if kind == "after":
                return [[band < bands - 1]] * halves
            slot = slot_of(kind, p)
            step = jnp.left_shift(1, slot // 2)
            there = t + jnp.where(slot % 2 == 0, -step, step)
            ok = (there >= 0) & (there < frames)
            live = density_ref[0, slot // 2]
            out = []
            for half in range(halves):
                row = []
                for kb in range(positions):
                    hit = (lists_ref[0, half, slot, 0] == kb) & (live > 0)
                    for i in range(1, positions):
                        hit = hit | ((lists_ref[0, half, slot, i] == kb) & (live > i))
                    row.append(ok & hit)
                out.append(row)
            return out

        rows_of = {
            "before": pl.ds(tokens - edge, edge),
            "after": pl.ds(0, edge),
            "other": pl.ds(pl.multiple_of(jnp.where(band > 0, tokens - edge, 0), edge), edge),
        }
        inner = (p > 0) & (p < GROUP - 1)
        bands_of = []
        for kind in kinds:
            allow = allow_of(kind)
            rows = (edge if kind in rows_of else tokens) // len(allow[0])
            for kb in range(len(allow[0])):
                row = bands_of[-1][0] + bands_of[-1][1] if bands_of else 0
                bands_of.append((row, rows, [allow[half][kb] for half in range(halves)]))

        def columns(h):
            return pl.ds(pl.multiple_of(h * HEAD_DIM, HEAD_DIM), HEAD_DIM)

        def stacked(h, part):
            cols = columns(h)
            pieces = []
            for i, kind in enumerate(kinds):
                rows = rows_of.get(kind, slice(None))
                refs_i = kv[starts[2 * i + part] : starts[2 * i + part + 1]]
                if kind == "GE" and part == 0:
                    whole, low, high = [ref[:, cols] for ref in refs_i]
                    high = jnp.where(inner, jnp.zeros_like(high), high)
                    piece = whole + join([low, high], 0)
                else:
                    piece = join([ref[rows, cols] for ref in refs_i], 0)
                pieces.append(piece)
            return join(pieces, 0)

        def scores(h, dst):
            s = contract(stacked(h, 0), q_ref[:, columns(h)], ((1,), (1,)))
            dst[...] = s
            tops = []
            for half in range(halves):
                cols = slice(half * edge, (half + 1) * edge)
                top = None if state is None else old_refs[0][h][:, cols]
                for row, rows, allow in bands_of:
                    piece = fold_max(s[row : row + rows, cols])
                    if allow[half] is not None:
                        piece = jnp.where(allow[half], piece, NEG)
                    top = piece if top is None else jnp.maximum(top, piece)
                tops.append(jnp.max(top, axis=0, keepdims=True))
            return join(tops, 1)

        def weigh(src, dst, top):
            for half in range(halves):
                cols = slice(half * edge, (half + 1) * edge)
                shift = top[:, cols] * SCALE2
                for row, rows, allow in bands_of:
                    off = shift if allow[half] is None else jnp.where(allow[half], shift, -NEG)
                    w = jnp.exp2(src[row : row + rows, cols] * SCALE2 - off)
                    dst[row : row + rows, cols] = w.astype(jnp.bfloat16)

        def mix(h, src, top):
            v = jnp.transpose(stacked(h, 1))
            ones = jnp.ones((2 * SUBLANES, v.shape[1]), jnp.bfloat16)
            mixed = contract(join([v, ones], 0), src[...], ((1,), (0,)))
            acc, total = mixed[:HEAD_DIM], mixed[HEAD_DIM : HEAD_DIM + SUBLANES]
            if state is not None:
                decay = jnp.exp2((old_refs[0][h][0:1] - top) * SCALE2)
                total = total + old_refs[1][h] * decay
                acc = acc + old_refs[2][h] * decay
            if final:
                scaled = acc * (1.0 / total[0:1])
                rest[0][:, columns(h)] = jnp.transpose(scaled.astype(jnp.bfloat16))
            else:
                rest[0][h] = jnp.broadcast_to(top, (SUBLANES, tokens))
                rest[1][h] = total
                rest[2][h] = acc

        s_refs, w_refs = scratch[:2], scratch[2:]

        def step(h, ready, next_ready, ahead):
            if ready is not None:
                for n in range(2):
                    mix(h + n, w_refs[n], ready[n])
            if next_ready is not None:
                for n in range(2):
                    weigh(s_refs[n], w_refs[n], next_ready[n])
            if ahead:
                return tuple(scores(h + 4 + n, s_refs[n]) for n in range(2))
            return None

        first = step(-4, None, None, True)
        second = step(-2, None, first, True)
        first, second = lax.fori_loop(
            0,
            heads // 2 - 2,
            lambda i, tops: (tops[1], step(2 * i, tops[0], tops[1], True)),
            (first, second),
            unroll=UNROLL,
        )
        step(heads - 4, first, second, False)
        step(heads - 2, second, None, False)

    smem = pl.BlockSpec(memory_space=pltpu.SMEM)
    vmem = pl.BlockSpec(memory_space=pltpu.VMEM)
    operands = [lists, density, q]
    keys = 0
    for kind, k, v in entries:
        operands += [*k, *v]
        keys += edge if kind in ("before", "after", "other") else tokens
    if state is not None:
        operands += list(state)
    operands = operands[:2] + [
        pltpu.with_memory_space_constraint(value, pltpu.VMEM) for value in operands[2:]
    ]
    specs = [smem, smem] + [vmem] * (len(operands) - 2)
    if final:
        outs, out_specs = jax.ShapeDtypeStruct((tokens, features), jnp.bfloat16), vmem
    else:
        small = pltpu.VMEM((heads, SUBLANES, tokens), jnp.float32)
        large = pltpu.VMEM((heads, HEAD_DIM, tokens), jnp.float32)
        outs, out_specs = (small, small, large), (vmem, vmem, vmem)
    return pl.pallas_call(
        kernel,
        in_specs=specs,
        out_specs=out_specs,
        out_shape=outs,
        scratch_shapes=[pltpu.VMEM((keys, tokens), jnp.float32)] * 2
        + [pltpu.VMEM((keys, tokens), jnp.bfloat16)] * 2,
        compiler_params=pltpu.CompilerParams(vmem_limit_bytes=VMEM_LIMIT),
        cost_estimate=pl.CostEstimate(
            flops=4 * tokens * keys * features,
            transcendentals=tokens * keys * heads,
            bytes_accessed=2 * features * (2 * keys + 4 * tokens),
        ),
    )(*operands)


def split_call(keys, values):
    half = keys.shape[1] // 2
    part = pltpu.VMEM((1, half) + keys.shape[2:], keys.dtype)

    def kernel(k_ref, v_ref, *rest):
        outs, sems = rest[:-1], rest[-1]
        sources = [
            k_ref.at[:, half:],
            k_ref.at[:, :half],
            v_ref.at[:, :half],
            v_ref.at[:, half:],
        ]
        copies = [
            pltpu.make_async_copy(src, dst, sems.at[n])
            for n, (src, dst) in enumerate(zip(sources, outs))
        ]
        for copy in copies:
            copy.start()
        for copy in copies:
            copy.wait()

    return pl.pallas_call(
        kernel,
        in_specs=[pl.BlockSpec(memory_space=pl.ANY)] * 2,
        out_specs=[pl.BlockSpec(memory_space=pltpu.VMEM)] * 4,
        out_shape=[part] * 4,
        compiler_params=pltpu.CompilerParams(vmem_limit_bytes=VMEM_LIMIT),
        scratch_shapes=[pltpu.SemaphoreType.DMA((4,))],
        name="split",
    )(keys, values)


def body(queries, keys, values, key_lists, density):
    _, rows_dev, width, features = queries.shape
    frames = lax.axis_size("tm")
    bands = lax.axis_size("space")
    route = routes(frames)
    up = [(i, i + 1) for i in range(bands - 1)]
    down = [(j, i) for i, j in up]

    def send(value, pairs, axis="tm"):
        return lax.ppermute(value, axis, pairs)

    def flat(value):
        return value.reshape(-1, features)

    b_k = send(keys, route["b"])
    x_k = send(keys, route["x"])
    x_v = send(values, route["x"])
    keys1, keys0, values0, values1 = split_call(keys, values)
    y_k1 = send(keys1, route["y"])
    y_v0 = send(values0, route["y"])
    y_v1 = send(values1, route["y"])
    y_k0 = send(keys0, route["y"])
    o_k0 = send(keys0, route["o"])
    o_k1 = send(keys1, route["o"])
    o_v = send(values, route["o"])
    if bands == 2:
        s_k = send(keys, up + down, "space")
        s_v = send(values, up + down, "space")
        beside = [("other", (flat(s_k),), (flat(s_v),))]
    else:
        up_k = send(keys, up, "space")
        up_v = send(values, up, "space")
        down_k = send(keys, down, "space")
        down_v = send(values, down, "space")
        beside = [
            ("before", (flat(up_k),), (flat(up_v),)),
            ("after", (flat(down_k),), (flat(down_v),)),
        ]

    p = lax.axis_index("tm") % GROUP
    inner = (p > 0) & (p < GROUP - 1)
    w_k1 = send(y_k1, route["b"])
    w_v0 = send(y_v0, route["b"])
    w_v1 = send(y_v1, route["b"])
    w_k0 = send(o_k0, route["y"])
    r_k = send(jnp.where(inner, w_k1, o_k0), route["x"])
    r_v0 = send(jnp.where(inner, w_v0, y_v0), route["x"])
    r_v1 = send(jnp.where(inner, w_v1, y_v1), route["x"])
    g_k = send(x_k, route["in_y"])
    b_v = send(values, route["b"])
    e_k0 = send(r_k, route["out_y"])

    q = flat(queries)
    state = stage_call(
        q,
        [("own", (flat(keys),), (flat(values),))] + beside,
        None,
        key_lists,
        density,
        False,
    )
    state = stage_call(
        q,
        [
            ("X", (flat(x_k),), (flat(x_v),)),
            ("Y", (flat(y_k0), flat(y_k1)), (flat(y_v0), flat(y_v1))),
        ],
        state,
        key_lists,
        density,
        False,
    )
    state = stage_call(
        q,
        [
            ("O", (flat(o_k0), flat(o_k1)), (flat(o_v),)),
            ("W", (flat(w_k0), flat(w_k1)), (flat(w_v0), flat(w_v1))),
        ],
        state,
        key_lists,
        density,
        False,
    )
    result = stage_call(
        q,
        [
            ("B", (flat(b_k),), (flat(b_v),)),
            ("GE", (flat(g_k), flat(e_k0), flat(r_k)), (flat(r_v0), flat(r_v1))),
        ],
        state,
        key_lists,
        density,
        True,
    )
    return result.reshape(1, rows_dev, width, features)


def solution(mesh):
    in_specs = (
        P("tm", "space", None, None),
        P("tm", "space", None, None),
        P("tm", "space", None, None),
        P("tm", "space", None, None),
        P("tm", None),
    )
    out_specs = P("tm", "space", None, None)
    return jax.shard_map(body, mesh=mesh, in_specs=in_specs, out_specs=out_specs, check_vma=False)
```

```python
import math

import jax
import jax.numpy as jnp
from jax import lax
from jax.experimental import pallas as pl
from jax.experimental.pallas import tpu as pltpu
from jax.sharding import PartitionSpec as P


HEAD_DIM = 128
OFFSETS = 3
GROUP = 2 ** (OFFSETS - 1)
SUBLANES = 8
UNROLL = 2
VMEM_LIMIT = 16 * 2**20
NEG = -1e30
SCALE2 = math.log2(math.e) / math.sqrt(HEAD_DIM)


def routes(count):
    def pairs(target):
        out = []
        for t in range(count):
            to = target(t, t % GROUP)
            if to is not None and 0 <= to < count:
                out.append((t, to))
        return out

    up = GROUP // 2
    return {
        "x": pairs(lambda t, p: t ^ 1),
        "y": pairs(lambda t, p: t ^ 2),
        "o": pairs(lambda t, p: t - GROUP if p < up else t + GROUP),
        "b": pairs(lambda t, p: t + GROUP if p < up else t - GROUP),
        "in_x": pairs(lambda t, p: t ^ 1 if p in (0, GROUP - 1) else None),
        "in_y": pairs(lambda t, p: t ^ 2 if p in (0, GROUP - 1) else None),
        "out_x": pairs(lambda t, p: t ^ 1 if p not in (0, GROUP - 1) else None),
        "out_y": pairs(lambda t, p: t ^ 2 if p not in (0, GROUP - 1) else None),
    }


def slot_of(name, p):
    low = (p < GROUP // 2).astype(jnp.int32)
    even = 1 - p % 2
    return {
        "X": even,
        "Y": 2 + low,
        "O": 4 + low,
        "B": 5 - low,
        "W": 3 - low,
        "GE": 1 - even,
    }[name]


def contract(a, b, dims):
    return lax.dot_general(a, b, (dims, ((), ())), preferred_element_type=jnp.float32)


def fold_max(value):
    return jnp.max(value.reshape(-1, SUBLANES, value.shape[1]), axis=0)


def join(parts, axis):
    return parts[0] if len(parts) == 1 else jnp.concatenate(parts, axis=axis)


def stage_call(q, entries, state, lists, density, final):
    tokens, features = q.shape
    heads = features // HEAD_DIM
    kinds = [entry[0] for entry in entries]
    starts = [0]
    for _, k, v in entries:
        starts += [starts[-1] + len(k), starts[-1] + len(k) + len(v)]
    halves = lists.shape[1]
    positions = lists.shape[2]
    frames = lax.axis_size("tm")
    bands = lax.axis_size("space")
    edge = tokens // halves
    n_in = starts[-1]

    def kernel(lists_ref, density_ref, *refs):
        q_ref = refs[0]
        kv = refs[1 : 1 + n_in]
        rest, scratch = refs[1 + n_in : -4], refs[-4:]
        old_refs = None
        if state is not None:
            old_refs = rest[:3]
            rest = rest[3:]
        t = lax.axis_index("tm")
        band = lax.axis_index("space")
        p = t % GROUP

        def allow_of(kind):
            if kind in ("own", "other"):
                return [[None]] * halves
            if kind == "before":
                return [[band > 0]] * halves
            if kind == "after":
                return [[band < bands - 1]] * halves
            slot = slot_of(kind, p)
            step = jnp.left_shift(1, slot // 2)
            there = t + jnp.where(slot % 2 == 0, -step, step)
            ok = (there >= 0) & (there < frames)
            live = density_ref[0, slot // 2]
            out = []
            for half in range(halves):
                row = []
                for kb in range(positions):
                    hit = (lists_ref[0, half, 0, slot] == kb) & (live > 0)
                    for i in range(1, positions):
                        hit = hit | ((lists_ref[0, half, i, slot] == kb) & (live > i))
                    row.append(ok & hit)
                out.append(row)
            return out

        rows_of = {
            "before": pl.ds(tokens - edge, edge),
            "after": pl.ds(0, edge),
            "other": pl.ds(pl.multiple_of(jnp.where(band > 0, tokens - edge, 0), edge), edge),
        }
        inner = is_inner(t)
        bands_of = []
        for kind in kinds:
            allow = allow_of(kind)
            rows = (edge if kind in rows_of else tokens) // len(allow[0])
            for kb in range(len(allow[0])):
                row = bands_of[-1][0] + bands_of[-1][1] if bands_of else 0
                bands_of.append((row, rows, [allow[half][kb] for half in range(halves)]))

        def columns(h):
            return pl.ds(pl.multiple_of(h * HEAD_DIM, HEAD_DIM), HEAD_DIM)

        def stacked(h, part):
            cols = columns(h)
            pieces = []
            for i, kind in enumerate(kinds):
                rows = rows_of.get(kind, slice(None))
                refs_i = kv[starts[2 * i + part] : starts[2 * i + part + 1]]
                if kind == "GE" and part == 0:
                    whole, low, high = [ref[:, cols] for ref in refs_i]
                    high = jnp.where(inner, jnp.zeros_like(high), high)
                    piece = whole + join([low, high], 0)
                else:
                    piece = join([ref[rows, cols] for ref in refs_i], 0)
                pieces.append(piece)
            return join(pieces, 0)

        def scores(h, dst):
            s = contract(stacked(h, 0), q_ref[:, columns(h)], ((1,), (1,)))
            dst[...] = s
            tops = []
            for half in range(halves):
                cols = slice(half * edge, (half + 1) * edge)
                top = None if state is None else old_refs[0][h][:, cols]
                for row, rows, allow in bands_of:
                    piece = fold_max(s[row : row + rows, cols])
                    if allow[half] is not None:
                        piece = jnp.where(allow[half], piece, NEG)
                    top = piece if top is None else jnp.maximum(top, piece)
                tops.append(jnp.max(top, axis=0, keepdims=True))
            return join(tops, 1)

        def weigh(src, dst, top):
            for half in range(halves):
                cols = slice(half * edge, (half + 1) * edge)
                shift = top[:, cols] * SCALE2
                for row, rows, allow in bands_of:
                    off = shift if allow[half] is None else jnp.where(allow[half], shift, -NEG)
                    w = jnp.exp2(src[row : row + rows, cols] * SCALE2 - off)
                    dst[row : row + rows, cols] = w.astype(jnp.bfloat16)

        def mix(h, src, top):
            v = jnp.transpose(stacked(h, 1))
            ones = jnp.ones((2 * SUBLANES, v.shape[1]), jnp.bfloat16)
            mixed = contract(join([v, ones], 0), src[...], ((1,), (0,)))
            acc, total = mixed[:HEAD_DIM], mixed[HEAD_DIM : HEAD_DIM + SUBLANES]
            if state is not None:
                decay = jnp.exp2((old_refs[0][h][0:1] - top) * SCALE2)
                total = total + old_refs[1][h] * decay
                acc = acc + old_refs[2][h] * decay
            if final:
                scaled = acc * (1.0 / total[0:1])
                rest[0][:, columns(h)] = jnp.transpose(scaled.astype(jnp.bfloat16))
            else:
                rest[0][h] = jnp.broadcast_to(top, (SUBLANES, tokens))
                rest[1][h] = total
                rest[2][h] = acc

        s_refs, w_refs = scratch[:2], scratch[2:]

        def step(h, ready, next_ready, ahead):
            if ready is not None:
                for n in range(2):
                    mix(h + n, w_refs[n], ready[n])
            if next_ready is not None:
                for n in range(2):
                    weigh(s_refs[n], w_refs[n], next_ready[n])
            if ahead:
                return tuple(scores(h + 4 + n, s_refs[n]) for n in range(2))
            return None

        first = step(-4, None, None, True)
        second = step(-2, None, first, True)
        first, second = lax.fori_loop(
            0,
            heads // 2 - 2,
            lambda i, tops: (tops[1], step(2 * i, tops[0], tops[1], True)),
            (first, second),
            unroll=UNROLL,
        )
        step(heads - 4, first, second, False)
        step(heads - 2, second, None, False)

    smem = pl.BlockSpec(memory_space=pltpu.SMEM)
    vmem = pl.BlockSpec(memory_space=pltpu.VMEM)
    operands = [lists, density, q]
    keys = 0
    for kind, k, v in entries:
        operands += [*k, *v]
        keys += edge if kind in ("before", "after", "other") else tokens
    if state is not None:
        operands += list(state)
    operands = operands[:2] + [
        pltpu.with_memory_space_constraint(value, pltpu.VMEM) for value in operands[2:]
    ]
    specs = [smem, smem] + [vmem] * (len(operands) - 2)
    if final:
        outs, out_specs = jax.ShapeDtypeStruct((tokens, features), jnp.bfloat16), vmem
    else:
        small = pltpu.VMEM((heads, SUBLANES, tokens), jnp.float32)
        large = pltpu.VMEM((heads, HEAD_DIM, tokens), jnp.float32)
        outs, out_specs = (small, small, large), (vmem, vmem, vmem)
    return pl.pallas_call(
        kernel,
        in_specs=specs,
        out_specs=out_specs,
        out_shape=outs,
        scratch_shapes=[pltpu.VMEM((keys, tokens), jnp.float32)] * 2
        + [pltpu.VMEM((keys, tokens), jnp.bfloat16)] * 2,
        compiler_params=pltpu.CompilerParams(vmem_limit_bytes=VMEM_LIMIT),
        cost_estimate=pl.CostEstimate(
            flops=4 * tokens * keys * features,
            transcendentals=tokens * keys * heads,
            bytes_accessed=2 * features * (2 * keys + 4 * tokens),
        ),
    )(*operands)


def is_inner(frame):
    p = frame % GROUP
    return (p > 0) & (p < GROUP - 1)


def pick_call(inner_value, outer_value):
    def kernel(inner_ref, outer_ref, out_ref):
        inner = is_inner(lax.axis_index("tm"))

        @pl.when(inner)
        def _():
            out_ref[...] = inner_ref[...]

        @pl.when(jnp.logical_not(inner))
        def _():
            out_ref[...] = outer_ref[...]

    vmem = pl.BlockSpec(memory_space=pltpu.VMEM)
    operands = [
        pltpu.with_memory_space_constraint(value, pltpu.VMEM)
        for value in (inner_value, outer_value)
    ]
    return pl.pallas_call(
        kernel,
        in_specs=[vmem, vmem],
        out_specs=vmem,
        out_shape=pltpu.VMEM(inner_value.shape, inner_value.dtype),
        compiler_params=pltpu.CompilerParams(vmem_limit_bytes=VMEM_LIMIT // 2),
        name="pick",
    )(*operands)


def split_call(value):
    half = value.shape[1] // 2
    part = pltpu.VMEM((1, half) + value.shape[2:], value.dtype)

    def kernel(ref, low, high, sems):
        copies = [
            pltpu.make_async_copy(ref.at[:, :half], low, sems.at[0]),
            pltpu.make_async_copy(ref.at[:, half:], high, sems.at[1]),
        ]
        for copy in copies:
            copy.start()
        for copy in copies:
            copy.wait()

    return pl.pallas_call(
        kernel,
        in_specs=[pl.BlockSpec(memory_space=pl.ANY)],
        out_specs=[pl.BlockSpec(memory_space=pltpu.VMEM)] * 2,
        out_shape=[part] * 2,
        scratch_shapes=[pltpu.SemaphoreType.DMA((2,))],
        compiler_params=pltpu.CompilerParams(vmem_limit_bytes=VMEM_LIMIT),
    )(value)


def body(queries, keys, values, key_lists, density):
    _, rows_dev, width, features = queries.shape
    frames = lax.axis_size("tm")
    bands = lax.axis_size("space")
    route = routes(frames)
    up = [(i, i + 1) for i in range(bands - 1)]
    down = [(j, i) for i, j in up]

    def send(value, pairs, axis="tm"):
        return lax.ppermute(value, axis, pairs)

    def flat(value):
        return value.reshape(-1, features)

    b_k = send(keys, route["b"])
    x_k = send(keys, route["x"])
    x_v = send(values, route["x"])
    keys0, keys1 = split_call(keys)
    values0, values1 = split_call(values)
    y_k1 = send(keys1, route["y"])
    y_v0 = send(values0, route["y"])
    y_v1 = send(values1, route["y"])
    y_k0 = send(keys0, route["y"])
    o_k0 = send(keys0, route["o"])
    o_k1 = send(keys1, route["o"])
    o_v = send(values, route["o"])
    if bands == 2:
        s_k = send(keys, up + down, "space")
        s_v = send(values, up + down, "space")
        beside = [("other", (flat(s_k),), (flat(s_v),))]
    else:
        up_k = send(keys, up, "space")
        up_v = send(values, up, "space")
        down_k = send(keys, down, "space")
        down_v = send(values, down, "space")
        beside = [
            ("before", (flat(up_k),), (flat(up_v),)),
            ("after", (flat(down_k),), (flat(down_v),)),
        ]

    w_k1 = send(y_k1, route["b"])
    w_v0 = send(y_v0, route["b"])
    w_v1 = send(y_v1, route["b"])
    w_k0 = send(o_k0, route["y"])
    r_k = send(pick_call(w_k1, o_k0), route["x"])
    r_v0 = send(pick_call(w_v0, y_v0), route["x"])
    r_v1 = send(pick_call(w_v1, y_v1), route["x"])
    g_k = send(x_k, route["in_y"])
    b_v = send(values, route["b"])
    e_k0 = send(r_k, route["out_y"])

    q = flat(queries)
    lists = jnp.swapaxes(key_lists, 2, 3)
    state = stage_call(
        q,
        [("own", (flat(keys0), flat(keys1)), (flat(values0), flat(values1)))]
        + beside
        + [
            ("X", (flat(x_k),), (flat(x_v),)),
            ("Y", (flat(y_k0), flat(y_k1)), (flat(y_v0), flat(y_v1))),
        ],
        None,
        lists,
        density,
        False,
    )
    state = stage_call(
        q,
        [
            ("O", (flat(o_k0), flat(o_k1)), (flat(o_v),)),
            ("W", (flat(w_k0), flat(w_k1)), (flat(w_v0), flat(w_v1))),
        ],
        state,
        lists,
        density,
        False,
    )
    state = stage_call(
        q,
        [("GE", (flat(g_k), flat(e_k0), flat(r_k)), (flat(r_v0), flat(r_v1)))],
        state,
        lists,
        density,
        False,
    )
    result = stage_call(
        q, [("B", (flat(b_k),), (flat(b_v),))], state, lists, density, True
    )
    return result.reshape(1, rows_dev, width, features)


def solution(mesh):
    in_specs = (
        P("tm", "space", None, None),
        P("tm", "space", None, None),
        P("tm", "space", None, None),
        P("tm", "space", None, None),
        P("tm", None),
    )
    out_specs = P("tm", "space", None, None)
    return jax.shard_map(body, mesh=mesh, in_specs=in_specs, out_specs=out_specs, check_vma=False)
```

```python
import math

import jax
import jax.numpy as jnp
from jax import lax
from jax.experimental import pallas as pl
from jax.experimental.pallas import tpu as pltpu
from jax.sharding import PartitionSpec as P


HEAD_DIM = 128
OFFSETS = 3
GROUP = 2 ** (OFFSETS - 1)
SUBLANES = 8
UNROLL = 2
LAST_UNROLL = 6
VMEM_LIMIT = 16 * 2**20
NEG = -1e30
SCALE2 = math.log2(math.e) / math.sqrt(HEAD_DIM)


def routes(count):
    def pairs(target):
        out = []
        for t in range(count):
            to = target(t, t % GROUP)
            if to is not None and 0 <= to < count:
                out.append((t, to))
        return out

    up = GROUP // 2
    return {
        "x": pairs(lambda t, p: t ^ 1),
        "y": pairs(lambda t, p: t ^ 2),
        "o": pairs(lambda t, p: t - GROUP if p < up else t + GROUP),
        "b": pairs(lambda t, p: t + GROUP if p < up else t - GROUP),
        "in_x": pairs(lambda t, p: t ^ 1 if p in (0, GROUP - 1) else None),
        "in_y": pairs(lambda t, p: t ^ 2 if p in (0, GROUP - 1) else None),
        "out_x": pairs(lambda t, p: t ^ 1 if p not in (0, GROUP - 1) else None),
        "out_y": pairs(lambda t, p: t ^ 2 if p not in (0, GROUP - 1) else None),
    }


def slot_of(name, p):
    low = (p < GROUP // 2).astype(jnp.int32)
    even = 1 - p % 2
    return {
        "X": even,
        "Y": 2 + low,
        "O": 4 + low,
        "B": 5 - low,
        "W": 3 - low,
        "GE": 1 - even,
    }[name]


def contract(a, b, dims):
    return lax.dot_general(a, b, (dims, ((), ())), preferred_element_type=jnp.float32)


def fold_max(value):
    return jnp.max(value.reshape(-1, SUBLANES, value.shape[1]), axis=0)


def join(parts, axis):
    return parts[0] if len(parts) == 1 else jnp.concatenate(parts, axis=axis)


def stage_call(q, entries, state, lists, density, ahead=()):
    tokens, features = q.shape
    heads = features // HEAD_DIM
    mixed_count = len(entries)
    entries = list(entries) + [(kind, k, ()) for kind, k in ahead]
    kinds = [entry[0] for entry in entries]
    starts = [0]
    for _, k, v in entries:
        starts += [starts[-1] + len(k), starts[-1] + len(k) + len(v)]
    halves = lists.shape[1]
    positions = lists.shape[2]
    frames = lax.axis_size("tm")
    bands = lax.axis_size("space")
    edge = tokens // halves
    n_in = starts[-1]

    def kernel(lists_ref, density_ref, *refs):
        q_ref = refs[0]
        kv = refs[1 : 1 + n_in]
        rest, scratch = refs[1 + n_in : -4], refs[-4:]
        old_refs = None
        if state is not None:
            old_refs = rest[:3]
            rest = rest[3:]
        t = lax.axis_index("tm")
        band = lax.axis_index("space")
        p = t % GROUP

        def allow_of(kind):
            if kind in ("own", "other"):
                return [[None]] * halves
            if kind == "before":
                return [[band > 0]] * halves
            if kind == "after":
                return [[band < bands - 1]] * halves
            slot = slot_of(kind, p)
            step = jnp.left_shift(1, slot // 2)
            there = t + jnp.where(slot % 2 == 0, -step, step)
            ok = (there >= 0) & (there < frames)
            live = density_ref[0, slot // 2]
            out = []
            for half in range(halves):
                row = []
                for kb in range(positions):
                    hit = (lists_ref[0, half, 0, slot] == kb) & (live > 0)
                    for i in range(1, positions):
                        hit = hit | ((lists_ref[0, half, i, slot] == kb) & (live > i))
                    row.append(ok & hit)
                out.append(row)
            return out

        rows_of = {
            "before": pl.ds(tokens - edge, edge),
            "after": pl.ds(0, edge),
            "other": pl.ds(pl.multiple_of(jnp.where(band > 0, tokens - edge, 0), edge), edge),
        }
        inner = is_inner(t)
        bands_of = []
        for kind in kinds:
            allow = allow_of(kind)
            rows = (edge if kind in rows_of else tokens) // len(allow[0])
            for kb in range(len(allow[0])):
                row = bands_of[-1][0] + bands_of[-1][1] if bands_of else 0
                bands_of.append((row, rows, [allow[half][kb] for half in range(halves)]))

        def columns(h):
            return pl.ds(pl.multiple_of(h * HEAD_DIM, HEAD_DIM), HEAD_DIM)

        def stacked(h, part):
            cols = columns(h)
            pieces = []
            for i, kind in enumerate(kinds if part == 0 else kinds[:mixed_count]):
                rows = rows_of.get(kind, slice(None))
                refs_i = kv[starts[2 * i + part] : starts[2 * i + part + 1]]
                if kind == "GE" and part == 0:
                    whole, low, high = [ref[:, cols] for ref in refs_i]
                    high = jnp.where(inner, jnp.zeros_like(high), high)
                    piece = whole + join([low, high], 0)
                else:
                    piece = join([ref[rows, cols] for ref in refs_i], 0)
                pieces.append(piece)
            return join(pieces, 0)

        def scores(h, dst):
            s = contract(stacked(h, 0), q_ref[:, columns(h)], ((1,), (1,)))
            dst[...] = s
            tops = []
            for half in range(halves):
                cols = slice(half * edge, (half + 1) * edge)
                top = None if state is None else old_refs[0][h][:, cols]
                for row, rows, allow in bands_of:
                    piece = fold_max(s[row : row + rows, cols])
                    if allow[half] is not None:
                        piece = jnp.where(allow[half], piece, NEG)
                    top = piece if top is None else jnp.maximum(top, piece)
                tops.append(jnp.max(top, axis=0, keepdims=True))
            return join(tops, 1)

        def weigh(h, src, dst, top):
            for half in range(halves):
                cols = slice(half * edge, (half + 1) * edge)
                shift = top[:, cols] * SCALE2
                for row, rows, allow in bands_of:
                    off = shift if allow[half] is None else jnp.where(allow[half], shift, -NEG)
                    w = jnp.exp2(src[row : row + rows, cols] * SCALE2 - off)
                    if row < keys:
                        dst[row : row + rows, cols] = w.astype(jnp.bfloat16)
                    else:
                        rest[3][h, row - keys : row - keys + rows, cols] = w.astype(jnp.bfloat16)

        def mix(h, src, top):
            v = jnp.transpose(stacked(h, 1))
            ones = jnp.ones((2 * SUBLANES, v.shape[1]), jnp.bfloat16)
            mixed = contract(join([v, ones], 0), src[...], ((1,), (0,)))
            acc, total = mixed[:HEAD_DIM], mixed[HEAD_DIM : HEAD_DIM + SUBLANES]
            if state is not None:
                decay = jnp.exp2((old_refs[0][h][0:1] - top) * SCALE2)
                total = total + old_refs[1][h] * decay
                acc = acc + old_refs[2][h] * decay
            rest[0][h] = jnp.broadcast_to(top, (SUBLANES, tokens))
            rest[1][h] = total
            rest[2][h] = acc

        s_refs, w_refs = scratch[:2], scratch[2:]

        def step(h, ready, next_ready, ahead):
            if ready is not None:
                for n in range(2):
                    mix(h + n, w_refs[n], ready[n])
            if next_ready is not None:
                for n in range(2):
                    weigh(h + 2 + n, s_refs[n], w_refs[n], next_ready[n])
            if ahead:
                return tuple(scores(h + 4 + n, s_refs[n]) for n in range(2))
            return None

        first = step(-4, None, None, True)
        second = step(-2, None, first, True)
        first, second = lax.fori_loop(
            0,
            heads // 2 - 2,
            lambda i, tops: (tops[1], step(2 * i, tops[0], tops[1], True)),
            (first, second),
            unroll=UNROLL,
        )
        step(heads - 4, first, second, False)
        step(heads - 2, second, None, False)

    smem = pl.BlockSpec(memory_space=pltpu.SMEM)
    vmem = pl.BlockSpec(memory_space=pltpu.VMEM)
    operands = [lists, density, q]
    keys = more = 0
    for kind, k, v in entries:
        operands += [*k, *v]
        count = edge if kind in ("before", "after", "other") else tokens
        keys, more = (keys + count, more) if len(v) > 0 else (keys, more + count)
    if state is not None:
        operands += list(state)
    operands = operands[:2] + [
        pltpu.with_memory_space_constraint(value, pltpu.VMEM) for value in operands[2:]
    ]
    specs = [smem, smem] + [vmem] * (len(operands) - 2)
    small = pltpu.VMEM((heads, SUBLANES, tokens), jnp.float32)
    large = pltpu.VMEM((heads, HEAD_DIM, tokens), jnp.float32)
    outs = [small, small, large]
    if more > 0:
        outs.append(pltpu.VMEM((heads, more, tokens), jnp.bfloat16))
    return pl.pallas_call(
        kernel,
        in_specs=specs,
        out_specs=[vmem] * len(outs),
        out_shape=outs,
        scratch_shapes=[pltpu.VMEM((keys + more, tokens), jnp.float32)] * 2
        + [pltpu.VMEM((keys, tokens), jnp.bfloat16)] * 2,
        compiler_params=pltpu.CompilerParams(vmem_limit_bytes=VMEM_LIMIT),
        cost_estimate=pl.CostEstimate(
            flops=4 * tokens * (keys + more) * features,
            transcendentals=tokens * keys * heads,
            bytes_accessed=2 * features * (2 * keys + 4 * tokens),
        ),
    )(*operands)


def last_call(value_rows, weights, weights_top, state):
    tokens, features = value_rows.shape
    heads = features // HEAD_DIM

    def kernel(v_ref, w_ref, w_top_ref, top_ref, total_ref, acc_ref, out_ref):
        def one_head(h, carry):
            cols = pl.ds(pl.multiple_of(h * HEAD_DIM, HEAD_DIM), HEAD_DIM)
            v = jnp.transpose(v_ref[:, cols])
            ones = jnp.ones((2 * SUBLANES, v.shape[1]), jnp.bfloat16)
            mixed = contract(join([v, ones], 0), w_ref[h], ((1,), (0,)))
            decay = jnp.exp2((w_top_ref[h][0:1] - top_ref[h][0:1]) * SCALE2)
            total = total_ref[h][0:1] + mixed[HEAD_DIM : HEAD_DIM + 1] * decay
            inverse = 1.0 / total
            acc = acc_ref[h] * inverse + mixed[:HEAD_DIM] * (decay * inverse)
            out_ref[:, cols] = jnp.transpose(acc.astype(jnp.bfloat16))
            return carry

        lax.fori_loop(0, heads, one_head, 0, unroll=LAST_UNROLL)

    vmem = pl.BlockSpec(memory_space=pltpu.VMEM)
    operands = [
        pltpu.with_memory_space_constraint(value, pltpu.VMEM)
        for value in (value_rows, weights, weights_top, *state)
    ]
    return pl.pallas_call(
        kernel,
        in_specs=[vmem] * len(operands),
        out_specs=vmem,
        out_shape=jax.ShapeDtypeStruct((tokens, features), jnp.bfloat16),
        compiler_params=pltpu.CompilerParams(vmem_limit_bytes=VMEM_LIMIT),
        name="last",
    )(*operands)


def is_inner(frame):
    p = frame % GROUP
    return (p > 0) & (p < GROUP - 1)


def pick_call(inner_value, outer_value):
    def kernel(inner_ref, outer_ref, out_ref):
        inner = is_inner(lax.axis_index("tm"))

        @pl.when(inner)
        def _():
            out_ref[...] = inner_ref[...]

        @pl.when(jnp.logical_not(inner))
        def _():
            out_ref[...] = outer_ref[...]

    vmem = pl.BlockSpec(memory_space=pltpu.VMEM)
    operands = [
        pltpu.with_memory_space_constraint(value, pltpu.VMEM)
        for value in (inner_value, outer_value)
    ]
    return pl.pallas_call(
        kernel,
        in_specs=[vmem, vmem],
        out_specs=vmem,
        out_shape=pltpu.VMEM(inner_value.shape, inner_value.dtype),
        compiler_params=pltpu.CompilerParams(vmem_limit_bytes=VMEM_LIMIT // 2),
        name="pick",
    )(*operands)


def split_call(value):
    half = value.shape[1] // 2
    part = pltpu.VMEM((1, half) + value.shape[2:], value.dtype)

    def kernel(ref, low, high, sems):
        copies = [
            pltpu.make_async_copy(ref.at[:, :half], low, sems.at[0]),
            pltpu.make_async_copy(ref.at[:, half:], high, sems.at[1]),
        ]
        for copy in copies:
            copy.start()
        for copy in copies:
            copy.wait()

    return pl.pallas_call(
        kernel,
        in_specs=[pl.BlockSpec(memory_space=pl.ANY)],
        out_specs=[pl.BlockSpec(memory_space=pltpu.VMEM)] * 2,
        out_shape=[part] * 2,
        scratch_shapes=[pltpu.SemaphoreType.DMA((2,))],
        compiler_params=pltpu.CompilerParams(vmem_limit_bytes=VMEM_LIMIT),
    )(value)


def body(queries, keys, values, key_lists, density):
    _, rows_dev, width, features = queries.shape
    frames = lax.axis_size("tm")
    bands = lax.axis_size("space")
    route = routes(frames)
    up = [(i, i + 1) for i in range(bands - 1)]
    down = [(j, i) for i, j in up]

    def send(value, pairs, axis="tm"):
        return lax.ppermute(value, axis, pairs)

    def flat(value):
        return value.reshape(-1, features)

    b_k = send(keys, route["b"])
    x_k = send(keys, route["x"])
    x_v = send(values, route["x"])
    keys0, keys1 = split_call(keys)
    values0, values1 = split_call(values)
    y_k1 = send(keys1, route["y"])
    y_v0 = send(values0, route["y"])
    y_v1 = send(values1, route["y"])
    y_k0 = send(keys0, route["y"])
    o_k0 = send(keys0, route["o"])
    o_k1 = send(keys1, route["o"])
    o_v = send(values, route["o"])
    if bands == 2:
        s_k = send(keys, up + down, "space")
        s_v = send(values, up + down, "space")
        beside = [("other", (flat(s_k),), (flat(s_v),))]
    else:
        up_k = send(keys, up, "space")
        up_v = send(values, up, "space")
        down_k = send(keys, down, "space")
        down_v = send(values, down, "space")
        beside = [
            ("before", (flat(up_k),), (flat(up_v),)),
            ("after", (flat(down_k),), (flat(down_v),)),
        ]

    w_k1 = send(y_k1, route["b"])
    w_v0 = send(y_v0, route["b"])
    w_v1 = send(y_v1, route["b"])
    w_k0 = send(o_k0, route["y"])
    r_k = send(pick_call(w_k1, o_k0), route["x"])
    r_v0 = send(pick_call(w_v0, y_v0), route["x"])
    r_v1 = send(pick_call(w_v1, y_v1), route["x"])
    g_k = send(x_k, route["in_y"])
    b_v = send(values, route["b"])
    e_k0 = send(r_k, route["out_y"])

    q = flat(queries)
    lists = jnp.swapaxes(key_lists, 2, 3)
    state = stage_call(
        q,
        [("own", (flat(keys0), flat(keys1)), (flat(values0), flat(values1)))]
        + beside
        + [
            ("X", (flat(x_k),), (flat(x_v),)),
            ("Y", (flat(y_k0), flat(y_k1)), (flat(y_v0), flat(y_v1))),
        ],
        None,
        lists,
        density,
    )
    *state, weights = stage_call(
        q,
        [
            ("O", (flat(o_k0), flat(o_k1)), (flat(o_v),)),
            ("W", (flat(w_k0), flat(w_k1)), (flat(w_v0), flat(w_v1))),
        ],
        state,
        lists,
        density,
        [("B", (flat(b_k),))],
    )
    weights_top = state[0]
    state = stage_call(
        q,
        [("GE", (flat(g_k), flat(e_k0), flat(r_k)), (flat(r_v0), flat(r_v1)))],
        state,
        lists,
        density,
    )
    result = last_call(flat(b_v), weights, weights_top, state)
    return result.reshape(1, rows_dev, width, features)


def solution(mesh):
    in_specs = (
        P("tm", "space", None, None),
        P("tm", "space", None, None),
        P("tm", "space", None, None),
        P("tm", "space", None, None),
        P("tm", None),
    )
    out_specs = P("tm", "space", None, None)
    return jax.shard_map(body, mesh=mesh, in_specs=in_specs, out_specs=out_specs, check_vma=False)
```

```python
import math

import jax
import jax.numpy as jnp
from jax import lax
from jax.experimental import pallas as pl
from jax.experimental.pallas import tpu as pltpu
from jax.sharding import PartitionSpec as P


HEAD_DIM = 128
OFFSETS = 3
GROUP = 2 ** (OFFSETS - 1)
SUBLANES = 8
UNROLL = 2
LAST_UNROLL = 12
VMEM_LIMIT = 16 * 2**20
NEG = -1e30
SCALE2 = math.log2(math.e) / math.sqrt(HEAD_DIM)


def routes(count):
    def pairs(target):
        out = []
        for t in range(count):
            to = target(t, t % GROUP)
            if to is not None and 0 <= to < count:
                out.append((t, to))
        return out

    up = GROUP // 2
    return {
        "x": pairs(lambda t, p: t ^ 1),
        "y": pairs(lambda t, p: t ^ 2),
        "o": pairs(lambda t, p: t - GROUP if p < up else t + GROUP),
        "b": pairs(lambda t, p: t + GROUP if p < up else t - GROUP),
        "in_x": pairs(lambda t, p: t ^ 1 if p in (0, GROUP - 1) else None),
        "in_y": pairs(lambda t, p: t ^ 2 if p in (0, GROUP - 1) else None),
        "out_x": pairs(lambda t, p: t ^ 1 if p not in (0, GROUP - 1) else None),
        "out_y": pairs(lambda t, p: t ^ 2 if p not in (0, GROUP - 1) else None),
    }


def slot_of(name, p):
    low = (p < GROUP // 2).astype(jnp.int32)
    even = 1 - p % 2
    return {
        "X": even,
        "Y": 2 + low,
        "O": 4 + low,
        "B": 5 - low,
        "W": 3 - low,
        "GE": 1 - even,
    }[name]


def contract(a, b, dims):
    return lax.dot_general(a, b, (dims, ((), ())), preferred_element_type=jnp.float32)


def fold_max(value):
    return jnp.max(value.reshape(-1, SUBLANES, value.shape[1]), axis=0)


def join(parts, axis):
    return parts[0] if len(parts) == 1 else jnp.concatenate(parts, axis=axis)


def stage_call(q, entries, state, lists, density, ahead=()):
    tokens, features = q.shape
    heads = features // HEAD_DIM
    mixed_count = len(entries)
    entries = list(entries) + [(kind, k, ()) for kind, k in ahead]
    kinds = [entry[0] for entry in entries]
    starts = [0]
    for _, k, v in entries:
        starts += [starts[-1] + len(k), starts[-1] + len(k) + len(v)]
    halves = lists.shape[1]
    positions = lists.shape[2]
    frames = lax.axis_size("tm")
    bands = lax.axis_size("space")
    edge = tokens // halves
    n_in = starts[-1]

    def kernel(lists_ref, density_ref, *refs):
        q_ref = refs[0]
        kv = refs[1 : 1 + n_in]
        rest, scratch = refs[1 + n_in : -4], refs[-4:]
        old_refs = None
        if state is not None:
            old_refs = rest[:3]
            rest = rest[3:]
        t = lax.axis_index("tm")
        band = lax.axis_index("space")
        p = t % GROUP

        def allow_of(kind):
            if kind in ("own", "other"):
                return [[None]] * halves
            if kind == "before":
                return [[band > 0]] * halves
            if kind == "after":
                return [[band < bands - 1]] * halves
            slot = slot_of(kind, p)
            step = jnp.left_shift(1, slot // 2)
            there = t + jnp.where(slot % 2 == 0, -step, step)
            ok = (there >= 0) & (there < frames)
            live = density_ref[0, slot // 2]
            out = []
            for half in range(halves):
                row = []
                for kb in range(positions):
                    hit = (lists_ref[0, half, 0, slot] == kb) & (live > 0)
                    for i in range(1, positions):
                        hit = hit | ((lists_ref[0, half, i, slot] == kb) & (live > i))
                    row.append(ok & hit)
                out.append(row)
            return out

        rows_of = {
            "before": pl.ds(tokens - edge, edge),
            "after": pl.ds(0, edge),
            "other": pl.ds(pl.multiple_of(jnp.where(band > 0, tokens - edge, 0), edge), edge),
        }
        inner = is_inner(t)
        bands_of = []
        for kind in kinds:
            allow = allow_of(kind)
            rows = (edge if kind in rows_of else tokens) // len(allow[0])
            for kb in range(len(allow[0])):
                row = bands_of[-1][0] + bands_of[-1][1] if bands_of else 0
                bands_of.append((row, rows, [allow[half][kb] for half in range(halves)]))

        def stacked(h, part):
            cols = columns(h)
            pieces = []
            for i, kind in enumerate(kinds if part == 0 else kinds[:mixed_count]):
                rows = rows_of.get(kind, slice(None))
                refs_i = kv[starts[2 * i + part] : starts[2 * i + part + 1]]
                if kind == "GE" and part == 0:
                    whole, low, high = [ref[:, cols] for ref in refs_i]
                    high = jnp.where(inner, jnp.zeros_like(high), high)
                    piece = whole + join([low, high], 0)
                else:
                    piece = join([ref[rows, cols] for ref in refs_i], 0)
                pieces.append(piece)
            return join(pieces, 0)

        def scores(h, dst):
            s = contract(stacked(h, 0), q_ref[:, columns(h)], ((1,), (1,)))
            dst[...] = s
            tops = []
            for half in range(halves):
                cols = slice(half * edge, (half + 1) * edge)
                top = None if state is None else old_refs[0][h][:, cols]
                for row, rows, allow in bands_of:
                    piece = fold_max(s[row : row + rows, cols])
                    if allow[half] is not None:
                        piece = jnp.where(allow[half], piece, NEG)
                    top = piece if top is None else jnp.maximum(top, piece)
                tops.append(jnp.max(top, axis=0, keepdims=True))
            return join(tops, 1)

        def weigh(h, src, dst, top):
            for half in range(halves):
                cols = slice(half * edge, (half + 1) * edge)
                shift = top[:, cols] * SCALE2
                for row, rows, allow in bands_of:
                    off = shift if allow[half] is None else jnp.where(allow[half], shift, -NEG)
                    w = jnp.exp2(src[row : row + rows, cols] * SCALE2 - off)
                    if row < keys:
                        dst[row : row + rows, cols] = w.astype(jnp.bfloat16)
                    else:
                        rest[3][h, row - keys : row - keys + rows, cols] = w.astype(jnp.bfloat16)

        def mix(h, src, top):
            v = jnp.transpose(stacked(h, 1))
            ones = jnp.ones((2 * SUBLANES, v.shape[1]), jnp.bfloat16)
            mixed = contract(join([v, ones], 0), src[...], ((1,), (0,)))
            acc, total = mixed[:HEAD_DIM], mixed[HEAD_DIM : HEAD_DIM + SUBLANES]
            if state is not None:
                decay = jnp.exp2((old_refs[0][h][0:1] - top) * SCALE2)
                total = total + old_refs[1][h] * decay
                acc = acc + old_refs[2][h] * decay
            rest[0][h] = jnp.broadcast_to(top, (SUBLANES, tokens))
            rest[1][h] = total
            rest[2][h] = acc

        s_refs, w_refs = scratch[:2], scratch[2:]

        def step(h, ready, next_ready, ahead):
            if ready is not None:
                for n in range(2):
                    mix(h + n, w_refs[n], ready[n])
            if next_ready is not None:
                for n in range(2):
                    weigh(h + 2 + n, s_refs[n], w_refs[n], next_ready[n])
            if ahead:
                return tuple(scores(h + 4 + n, s_refs[n]) for n in range(2))
            return None

        first = step(-4, None, None, True)
        second = step(-2, None, first, True)
        first, second = lax.fori_loop(
            0,
            heads // 2 - 2,
            lambda i, tops: (tops[1], step(2 * i, tops[0], tops[1], True)),
            (first, second),
            unroll=UNROLL,
        )
        step(heads - 4, first, second, False)
        step(heads - 2, second, None, False)

    smem = pl.BlockSpec(memory_space=pltpu.SMEM)
    vmem = pl.BlockSpec(memory_space=pltpu.VMEM)
    operands = [lists, density, q]
    keys = more = 0
    for kind, k, v in entries:
        operands += [*k, *v]
        count = edge if kind in ("before", "after", "other") else tokens
        keys, more = (keys + count, more) if len(v) > 0 else (keys, more + count)
    if state is not None:
        operands += list(state)
    operands = operands[:2] + [
        pltpu.with_memory_space_constraint(value, pltpu.VMEM) for value in operands[2:]
    ]
    specs = [smem, smem] + [vmem] * (len(operands) - 2)
    small = pltpu.VMEM((heads, SUBLANES, tokens), jnp.float32)
    large = pltpu.VMEM((heads, HEAD_DIM, tokens), jnp.float32)
    outs = [small, small, large]
    if more > 0:
        outs.append(pltpu.VMEM((heads, more, tokens), jnp.bfloat16))
    return pl.pallas_call(
        kernel,
        in_specs=specs,
        out_specs=[vmem] * len(outs),
        out_shape=outs,
        scratch_shapes=[pltpu.VMEM((keys + more, tokens), jnp.float32)] * 2
        + [pltpu.VMEM((keys, tokens), jnp.bfloat16)] * 2,
        compiler_params=pltpu.CompilerParams(vmem_limit_bytes=VMEM_LIMIT),
        cost_estimate=pl.CostEstimate(
            flops=4 * tokens * (keys + more) * features,
            transcendentals=tokens * keys * heads,
            bytes_accessed=2 * features * (2 * keys + 4 * tokens),
        ),
    )(*operands)


def columns(h):
    return pl.ds(pl.multiple_of(h * HEAD_DIM, HEAD_DIM), HEAD_DIM)


def last_call(value_rows, weights, weights_top, state):
    tokens, features = value_rows.shape
    heads = features // HEAD_DIM

    def kernel(v_ref, w_ref, w_top_ref, top_ref, total_ref, acc_ref, out_ref, done_ref, sems):
        def leave(h):
            cols = columns(h)
            return pltpu.make_async_copy(done_ref.at[:, cols], out_ref.at[:, cols], sems.at[h])

        def one_head(h, carry):
            cols = columns(h)
            v = jnp.transpose(v_ref[:, cols])
            ones = jnp.ones((2 * SUBLANES, v.shape[1]), jnp.bfloat16)
            mixed = contract(join([v, ones], 0), w_ref[h], ((1,), (0,)))
            decay = jnp.exp2((w_top_ref[h][0:1] - top_ref[h][0:1]) * SCALE2)
            total = total_ref[h][0:1] + mixed[HEAD_DIM : HEAD_DIM + 1] * decay
            inverse = 1.0 / total
            acc = acc_ref[h] * inverse + mixed[:HEAD_DIM] * (decay * inverse)
            done_ref[:, cols] = jnp.transpose(acc.astype(jnp.bfloat16))
            leave(h).start()
            return carry

        lax.fori_loop(0, heads, one_head, 0, unroll=LAST_UNROLL)
        for h in range(heads):
            leave(h).wait()

    vmem = pl.BlockSpec(memory_space=pltpu.VMEM)
    operands = [
        pltpu.with_memory_space_constraint(value, pltpu.VMEM)
        for value in (value_rows, weights, weights_top, *state)
    ]
    return pl.pallas_call(
        kernel,
        in_specs=[vmem] * len(operands),
        out_specs=pl.BlockSpec(memory_space=pl.ANY),
        out_shape=jax.ShapeDtypeStruct((tokens, features), jnp.bfloat16),
        scratch_shapes=[
            pltpu.VMEM((tokens, features), jnp.bfloat16),
            pltpu.SemaphoreType.DMA((heads,)),
        ],
        compiler_params=pltpu.CompilerParams(vmem_limit_bytes=VMEM_LIMIT),
        name="last",
    )(*operands)


def is_inner(frame):
    p = frame % GROUP
    return (p > 0) & (p < GROUP - 1)


def pick_call(inner_value, outer_value):
    def kernel(inner_ref, outer_ref, out_ref):
        inner = is_inner(lax.axis_index("tm"))

        @pl.when(inner)
        def _():
            out_ref[...] = inner_ref[...]

        @pl.when(jnp.logical_not(inner))
        def _():
            out_ref[...] = outer_ref[...]

    vmem = pl.BlockSpec(memory_space=pltpu.VMEM)
    operands = [
        pltpu.with_memory_space_constraint(value, pltpu.VMEM)
        for value in (inner_value, outer_value)
    ]
    return pl.pallas_call(
        kernel,
        in_specs=[vmem, vmem],
        out_specs=vmem,
        out_shape=pltpu.VMEM(inner_value.shape, inner_value.dtype),
        compiler_params=pltpu.CompilerParams(vmem_limit_bytes=VMEM_LIMIT // 2),
        name="pick",
    )(*operands)


def split_call(value):
    half = value.shape[1] // 2
    part = pltpu.VMEM((1, half) + value.shape[2:], value.dtype)

    def kernel(ref, low, high, sems):
        copies = [
            pltpu.make_async_copy(ref.at[:, :half], low, sems.at[0]),
            pltpu.make_async_copy(ref.at[:, half:], high, sems.at[1]),
        ]
        for copy in copies:
            copy.start()
        for copy in copies:
            copy.wait()

    return pl.pallas_call(
        kernel,
        in_specs=[pl.BlockSpec(memory_space=pl.ANY)],
        out_specs=[pl.BlockSpec(memory_space=pltpu.VMEM)] * 2,
        out_shape=[part] * 2,
        scratch_shapes=[pltpu.SemaphoreType.DMA((2,))],
        compiler_params=pltpu.CompilerParams(vmem_limit_bytes=VMEM_LIMIT),
    )(value)


def body(queries, keys, values, key_lists, density):
    _, rows_dev, width, features = queries.shape
    frames = lax.axis_size("tm")
    bands = lax.axis_size("space")
    route = routes(frames)
    up = [(i, i + 1) for i in range(bands - 1)]
    down = [(j, i) for i, j in up]

    def send(value, pairs, axis="tm"):
        return lax.ppermute(value, axis, pairs)

    def flat(value):
        return value.reshape(-1, features)

    b_k = send(keys, route["b"])
    x_k = send(keys, route["x"])
    x_v = send(values, route["x"])
    keys0, keys1 = split_call(keys)
    values0, values1 = split_call(values)
    y_k1 = send(keys1, route["y"])
    y_v0 = send(values0, route["y"])
    y_v1 = send(values1, route["y"])
    y_k0 = send(keys0, route["y"])
    o_k0 = send(keys0, route["o"])
    o_k1 = send(keys1, route["o"])
    o_v = send(values, route["o"])
    if bands == 2:
        s_k = send(keys, up + down, "space")
        s_v = send(values, up + down, "space")
        beside = [("other", (flat(s_k),), (flat(s_v),))]
    else:
        up_k = send(keys, up, "space")
        up_v = send(values, up, "space")
        down_k = send(keys, down, "space")
        down_v = send(values, down, "space")
        beside = [
            ("before", (flat(up_k),), (flat(up_v),)),
            ("after", (flat(down_k),), (flat(down_v),)),
        ]

    w_k1 = send(y_k1, route["b"])
    w_v0 = send(y_v0, route["b"])
    w_v1 = send(y_v1, route["b"])
    w_k0 = send(o_k0, route["y"])
    r_k = send(pick_call(w_k1, o_k0), route["x"])
    r_v0 = send(pick_call(w_v0, y_v0), route["x"])
    r_v1 = send(pick_call(w_v1, y_v1), route["x"])
    g_k = send(x_k, route["in_y"])
    b_v = send(values, route["b"])
    e_k0 = send(r_k, route["out_y"])

    q = flat(queries)
    lists = jnp.swapaxes(key_lists, 2, 3)
    state = stage_call(
        q,
        [("own", (flat(keys0), flat(keys1)), (flat(values0), flat(values1)))]
        + beside
        + [
            ("X", (flat(x_k),), (flat(x_v),)),
            ("Y", (flat(y_k0), flat(y_k1)), (flat(y_v0), flat(y_v1))),
        ],
        None,
        lists,
        density,
    )
    *state, weights = stage_call(
        q,
        [
            ("O", (flat(o_k0), flat(o_k1)), (flat(o_v),)),
            ("W", (flat(w_k0), flat(w_k1)), (flat(w_v0), flat(w_v1))),
        ],
        state,
        lists,
        density,
        [("B", (flat(b_k),))],
    )
    weights_top = state[0]
    state = stage_call(
        q,
        [("GE", (flat(g_k), flat(e_k0), flat(r_k)), (flat(r_v0), flat(r_v1)))],
        state,
        lists,
        density,
    )
    result = last_call(flat(b_v), weights, weights_top, state)
    return result.reshape(1, rows_dev, width, features)


def solution(mesh):
    in_specs = (
        P("tm", "space", None, None),
        P("tm", "space", None, None),
        P("tm", "space", None, None),
        P("tm", "space", None, None),
        P("tm", None),
    )
    out_specs = P("tm", "space", None, None)
    return jax.shard_map(body, mesh=mesh, in_specs=in_specs, out_specs=out_specs, check_vma=False)
```

```python
import math

import jax
import jax.numpy as jnp
from jax import lax
from jax.experimental import pallas as pl
from jax.experimental.pallas import tpu as pltpu
from jax.sharding import PartitionSpec as P


HEAD_DIM = 128
OFFSETS = 3
GROUP = 2 ** (OFFSETS - 1)
SUBLANES = 8
UNROLL = 2
LAST_UNROLL = 12
VMEM_LIMIT = 16 * 2**20
NEG = -1e30
SCALE2 = math.log2(math.e) / math.sqrt(HEAD_DIM)


def routes(count):
    def pairs(target):
        out = []
        for t in range(count):
            to = target(t, t % GROUP)
            if to is not None and 0 <= to < count:
                out.append((t, to))
        return out

    up = GROUP // 2
    return {
        "x": pairs(lambda t, p: t ^ 1),
        "y": pairs(lambda t, p: t ^ 2),
        "o": pairs(lambda t, p: t - GROUP if p < up else t + GROUP),
        "b": pairs(lambda t, p: t + GROUP if p < up else t - GROUP),
        "in_x": pairs(lambda t, p: t ^ 1 if p in (0, GROUP - 1) else None),
        "in_y": pairs(lambda t, p: t ^ 2 if p in (0, GROUP - 1) else None),
        "out_x": pairs(lambda t, p: t ^ 1 if p not in (0, GROUP - 1) else None),
        "out_y": pairs(lambda t, p: t ^ 2 if p not in (0, GROUP - 1) else None),
    }


def slot_of(name, p):
    low = (p < GROUP // 2).astype(jnp.int32)
    even = 1 - p % 2
    return {
        "X": even,
        "Y": 2 + low,
        "O": 4 + low,
        "B": 5 - low,
        "W": 3 - low,
        "GE": 1 - even,
    }[name]


def contract(a, b, dims):
    return lax.dot_general(a, b, (dims, ((), ())), preferred_element_type=jnp.float32)


def fold_max(value):
    return jnp.max(value.reshape(-1, SUBLANES, value.shape[1]), axis=0)


def join(parts, axis):
    return parts[0] if len(parts) == 1 else jnp.concatenate(parts, axis=axis)


def stage_call(q, entries, state, lists, density, ahead=()):
    tokens, features = q.shape
    heads = features // HEAD_DIM
    mixed_count = len(entries)
    entries = list(entries) + [(kind, k, ()) for kind, k in ahead]
    kinds = [entry[0] for entry in entries]
    starts = [0]
    for _, k, v in entries:
        starts += [starts[-1] + len(k), starts[-1] + len(k) + len(v)]
    halves = lists.shape[1]
    positions = lists.shape[2]
    frames = lax.axis_size("tm")
    bands = lax.axis_size("space")
    edge = tokens // halves
    n_in = starts[-1]

    def kernel(lists_ref, density_ref, *refs):
        q_ref = refs[0]
        kv = refs[1 : 1 + n_in]
        rest, scratch = refs[1 + n_in : -4], refs[-4:]
        old_refs = None
        if state is not None:
            old_refs = rest[:3]
            rest = rest[3:]
        t = lax.axis_index("tm")
        band = lax.axis_index("space")
        p = t % GROUP

        def allow_of(kind):
            if kind in ("own", "other"):
                return [[None]] * halves
            if kind == "before":
                return [[band > 0]] * halves
            if kind == "after":
                return [[band < bands - 1]] * halves
            slot = slot_of(kind, p)
            step = jnp.left_shift(1, slot // 2)
            there = t + jnp.where(slot % 2 == 0, -step, step)
            ok = (there >= 0) & (there < frames)
            live = density_ref[0, slot // 2]
            out = []
            for half in range(halves):
                row = []
                for kb in range(positions):
                    hit = (lists_ref[0, half, 0, slot] == kb) & (live > 0)
                    for i in range(1, positions):
                        hit = hit | ((lists_ref[0, half, i, slot] == kb) & (live > i))
                    row.append(ok & hit)
                out.append(row)
            return out

        rows_of = {
            "before": pl.ds(tokens - edge, edge),
            "after": pl.ds(0, edge),
            "other": pl.ds(pl.multiple_of(jnp.where(band > 0, tokens - edge, 0), edge), edge),
        }
        inner = is_inner(t)
        bands_of = []
        for kind in kinds:
            allow = allow_of(kind)
            rows = (edge if kind in rows_of else tokens) // len(allow[0])
            for kb in range(len(allow[0])):
                row = bands_of[-1][0] + bands_of[-1][1] if bands_of else 0
                bands_of.append((row, rows, [allow[half][kb] for half in range(halves)]))

        def stacked(h, part):
            cols = columns(h)
            pieces = []
            for i, kind in enumerate(kinds if part == 0 else kinds[:mixed_count]):
                rows = rows_of.get(kind, slice(None))
                refs_i = kv[starts[2 * i + part] : starts[2 * i + part + 1]]
                if kind == "GE" and part == 0:
                    whole, low, high = [ref[:, cols] for ref in refs_i]
                    high = high[: tokens - low.shape[0]]
                    high = jnp.where(inner, jnp.zeros_like(high), high)
                    piece = whole + join([low, high], 0)
                else:
                    piece = join([ref[rows, cols] for ref in refs_i], 0)
                pieces.append(piece)
            return join(pieces, 0)

        def scores(h, dst):
            s = contract(stacked(h, 0), q_ref[:, columns(h)], ((1,), (1,)))
            dst[...] = s
            tops = []
            for half in range(halves):
                cols = slice(half * edge, (half + 1) * edge)
                top = None if state is None else old_refs[0][h][:, cols]
                for row, rows, allow in bands_of:
                    piece = fold_max(s[row : row + rows, cols])
                    if allow[half] is not None:
                        piece = jnp.where(allow[half], piece, NEG)
                    top = piece if top is None else jnp.maximum(top, piece)
                tops.append(jnp.max(top, axis=0, keepdims=True))
            return join(tops, 1)

        def weigh(h, src, dst, top):
            for half in range(halves):
                cols = slice(half * edge, (half + 1) * edge)
                shift = top[:, cols] * SCALE2
                for row, rows, allow in bands_of:
                    off = shift if allow[half] is None else jnp.where(allow[half], shift, -NEG)
                    w = jnp.exp2(src[row : row + rows, cols] * SCALE2 - off)
                    if row < keys:
                        dst[row : row + rows, cols] = w.astype(jnp.bfloat16)
                    else:
                        rest[-1][h, row - keys : row - keys + rows, cols] = w.astype(jnp.bfloat16)

        def mix(h, src, top):
            rest[0][h] = jnp.broadcast_to(top, (SUBLANES, tokens))
            if mixed_count == 0:
                return
            v = jnp.transpose(stacked(h, 1))
            ones = jnp.ones((2 * SUBLANES, v.shape[1]), jnp.bfloat16)
            mixed = contract(join([v, ones], 0), src[...], ((1,), (0,)))
            acc, total = mixed[:HEAD_DIM], mixed[HEAD_DIM : HEAD_DIM + SUBLANES]
            if state is not None:
                decay = jnp.exp2((old_refs[0][h][0:1] - top) * SCALE2)
                total = total + old_refs[1][h] * decay
                acc = acc + old_refs[2][h] * decay
            rest[1][h] = total
            rest[2][h] = acc

        s_refs, w_refs = scratch[:2], scratch[2:]

        def step(h, ready, next_ready, ahead):
            if ready is not None:
                for n in range(2):
                    mix(h + n, w_refs[n], ready[n])
            if next_ready is not None:
                for n in range(2):
                    weigh(h + 2 + n, s_refs[n], w_refs[n], next_ready[n])
            if ahead:
                return tuple(scores(h + 4 + n, s_refs[n]) for n in range(2))
            return None

        first = step(-4, None, None, True)
        second = step(-2, None, first, True)
        first, second = lax.fori_loop(
            0,
            heads // 2 - 2,
            lambda i, tops: (tops[1], step(2 * i, tops[0], tops[1], True)),
            (first, second),
            unroll=UNROLL,
        )
        step(heads - 4, first, second, False)
        step(heads - 2, second, None, False)

    smem = pl.BlockSpec(memory_space=pltpu.SMEM)
    vmem = pl.BlockSpec(memory_space=pltpu.VMEM)
    operands = [lists, density, q]
    keys = more = 0
    for kind, k, v in entries:
        operands += [*k, *v]
        count = edge if kind in ("before", "after", "other") else tokens
        keys, more = (keys + count, more) if len(v) > 0 else (keys, more + count)
    if state is not None:
        operands += list(state)
    operands = operands[:2] + [
        pltpu.with_memory_space_constraint(value, pltpu.VMEM) for value in operands[2:]
    ]
    specs = [smem, smem] + [vmem] * (len(operands) - 2)
    small = pltpu.VMEM((heads, SUBLANES, tokens), jnp.float32)
    large = pltpu.VMEM((heads, HEAD_DIM, tokens), jnp.float32)
    outs = [small, small, large] if keys > 0 else [small]
    if more > 0:
        outs.append(pltpu.VMEM((heads, more, tokens), jnp.bfloat16))
    return pl.pallas_call(
        kernel,
        in_specs=specs,
        out_specs=[vmem] * len(outs),
        out_shape=outs,
        scratch_shapes=[pltpu.VMEM((keys + more, tokens), jnp.float32)] * 2
        + [pltpu.VMEM((max(keys, tokens), tokens), jnp.bfloat16)] * 2,
        compiler_params=pltpu.CompilerParams(vmem_limit_bytes=VMEM_LIMIT),
        cost_estimate=pl.CostEstimate(
            flops=4 * tokens * (keys + more) * features,
            transcendentals=tokens * keys * heads,
            bytes_accessed=2 * features * (2 * keys + 4 * tokens),
        ),
    )(*operands)


def columns(h):
    return pl.ds(pl.multiple_of(h * HEAD_DIM, HEAD_DIM), HEAD_DIM)


def blend_call(value_parts, weights, top, state):
    _, old_total, old_acc = state
    heads = old_acc.shape[0]
    count = len(value_parts)

    def kernel(*refs):
        v_refs = refs[:count]
        w_ref, top_ref, old_top_ref, old_total_ref, old_acc_ref, total_ref, acc_ref = refs[count:]

        def one_head(h, carry):
            cols = columns(h)
            v = jnp.transpose(join([ref[:, cols] for ref in v_refs], 0))
            ones = jnp.ones((2 * SUBLANES, v.shape[1]), jnp.bfloat16)
            mixed = contract(join([v, ones], 0), w_ref[h], ((1,), (0,)))
            decay = jnp.exp2((old_top_ref[h][0:1] - top_ref[h][0:1]) * SCALE2)
            total_ref[h] = old_total_ref[h] * decay + mixed[HEAD_DIM : HEAD_DIM + SUBLANES]
            acc_ref[h] = old_acc_ref[h] * decay + mixed[:HEAD_DIM]
            return carry

        lax.fori_loop(0, heads, one_head, 0, unroll=LAST_UNROLL)

    vmem = pl.BlockSpec(memory_space=pltpu.VMEM)
    operands = [
        pltpu.with_memory_space_constraint(value, pltpu.VMEM)
        for value in (*value_parts, weights, top, *state)
    ]
    return pl.pallas_call(
        kernel,
        in_specs=[vmem] * len(operands),
        out_specs=[vmem] * 2,
        out_shape=[
            pltpu.VMEM(old_total.shape, jnp.float32),
            pltpu.VMEM(old_acc.shape, jnp.float32),
        ],
        compiler_params=pltpu.CompilerParams(vmem_limit_bytes=VMEM_LIMIT),
        name="blend",
    )(*operands)


def last_call(value_rows, weights, weights_top, state):
    tokens, features = value_rows.shape
    heads = features // HEAD_DIM

    def kernel(v_ref, w_ref, w_top_ref, top_ref, total_ref, acc_ref, out_ref, done_ref, sems):
        def leave(h):
            cols = columns(h)
            return pltpu.make_async_copy(done_ref.at[:, cols], out_ref.at[:, cols], sems.at[h])

        def one_head(h, carry):
            cols = columns(h)
            v = jnp.transpose(v_ref[:, cols])
            ones = jnp.ones((2 * SUBLANES, v.shape[1]), jnp.bfloat16)
            mixed = contract(join([v, ones], 0), w_ref[h], ((1,), (0,)))
            decay = jnp.exp2((w_top_ref[h][0:1] - top_ref[h][0:1]) * SCALE2)
            total = total_ref[h][0:1] + mixed[HEAD_DIM : HEAD_DIM + 1] * decay
            inverse = 1.0 / total
            acc = acc_ref[h] * inverse + mixed[:HEAD_DIM] * (decay * inverse)
            done_ref[:, cols] = jnp.transpose(acc.astype(jnp.bfloat16))
            leave(h).start()
            return carry

        lax.fori_loop(0, heads, one_head, 0, unroll=LAST_UNROLL)
        for h in range(heads):
            leave(h).wait()

    vmem = pl.BlockSpec(memory_space=pltpu.VMEM)
    operands = [
        pltpu.with_memory_space_constraint(value, pltpu.VMEM)
        for value in (value_rows, weights, weights_top, *state)
    ]
    return pl.pallas_call(
        kernel,
        in_specs=[vmem] * len(operands),
        out_specs=pl.BlockSpec(memory_space=pl.ANY),
        out_shape=jax.ShapeDtypeStruct((tokens, features), jnp.bfloat16),
        scratch_shapes=[
            pltpu.VMEM((tokens, features), jnp.bfloat16),
            pltpu.SemaphoreType.DMA((heads,)),
        ],
        compiler_params=pltpu.CompilerParams(vmem_limit_bytes=VMEM_LIMIT),
        name="last",
    )(*operands)


def is_inner(frame):
    p = frame % GROUP
    return (p > 0) & (p < GROUP - 1)


def pick_call(inner_value, outer_value):
    rows = inner_value.shape[0]

    def kernel(inner_ref, outer_ref, out_ref):
        inner = is_inner(lax.axis_index("tm"))

        @pl.when(inner)
        def _():
            out_ref[:rows] = inner_ref[...]
            if rows < out_ref.shape[0]:
                out_ref[rows:] = jnp.zeros_like(out_ref[rows:])

        @pl.when(jnp.logical_not(inner))
        def _():
            out_ref[...] = outer_ref[...]

    vmem = pl.BlockSpec(memory_space=pltpu.VMEM)
    operands = [
        pltpu.with_memory_space_constraint(value, pltpu.VMEM)
        for value in (inner_value, outer_value)
    ]
    return pl.pallas_call(
        kernel,
        in_specs=[vmem, vmem],
        out_specs=vmem,
        out_shape=pltpu.VMEM(outer_value.shape, outer_value.dtype),
        compiler_params=pltpu.CompilerParams(vmem_limit_bytes=VMEM_LIMIT // 2),
        name="pick",
    )(*operands)


def split_call(value, cut):
    rows, features = value.shape
    parts = [pltpu.VMEM((size, features), value.dtype) for size in (cut, rows - cut)]

    def kernel(ref, low, high, sems):
        copies = [
            pltpu.make_async_copy(ref.at[:cut], low, sems.at[0]),
            pltpu.make_async_copy(ref.at[cut:], high, sems.at[1]),
        ]
        for copy in copies:
            copy.start()
        for copy in copies:
            copy.wait()

    return pl.pallas_call(
        kernel,
        in_specs=[pl.BlockSpec(memory_space=pl.ANY)],
        out_specs=[pl.BlockSpec(memory_space=pltpu.VMEM)] * 2,
        out_shape=parts,
        scratch_shapes=[pltpu.SemaphoreType.DMA((2,))],
        compiler_params=pltpu.CompilerParams(vmem_limit_bytes=VMEM_LIMIT),
    )(value)


def body(queries, keys, values, key_lists, density):
    _, rows_dev, width, features = queries.shape
    tokens = rows_dev * width
    frames = lax.axis_size("tm")
    bands = lax.axis_size("space")
    route = routes(frames)
    up = [(i, i + 1) for i in range(bands - 1)]
    down = [(j, i) for i, j in up]

    def send(value, pairs, axis="tm"):
        return lax.ppermute(value, axis, pairs)

    def flat(value):
        return value.reshape(-1, features)

    b_k = send(keys, route["b"])
    x_k = send(keys, route["x"])
    x_v = send(values, route["x"])
    keys0, keys1 = split_call(flat(keys), tokens * 17 // 32)
    values0, values1 = split_call(flat(values), tokens // 2)
    y_k1 = send(keys1, route["y"])
    y_v0 = send(values0, route["y"])
    y_v1 = send(values1, route["y"])
    y_k0 = send(keys0, route["y"])
    o_k0 = send(keys0, route["o"])
    o_k1 = send(keys1, route["o"])
    o_v = send(values, route["o"])
    if bands == 2:
        s_k = send(keys, up + down, "space")
        s_v = send(values, up + down, "space")
        beside = [("other", (flat(s_k),), (flat(s_v),))]
    else:
        up_k = send(keys, up, "space")
        up_v = send(values, up, "space")
        down_k = send(keys, down, "space")
        down_v = send(values, down, "space")
        beside = [
            ("before", (flat(up_k),), (flat(up_v),)),
            ("after", (flat(down_k),), (flat(down_v),)),
        ]

    w_k1 = send(y_k1, route["b"])
    w_v0 = send(y_v0, route["b"])
    w_v1 = send(y_v1, route["b"])
    w_k0 = send(o_k0, route["y"])
    r_k = send(pick_call(w_k1, o_k0), route["x"])
    r_v0 = send(pick_call(w_v0, y_v0), route["x"])
    r_v1 = send(pick_call(w_v1, y_v1), route["x"])
    g_k = send(x_k, route["in_y"])
    b_v = send(values, route["b"])
    e_k0 = send(r_k, route["out_y"])

    q = flat(queries)
    lists = jnp.swapaxes(key_lists, 2, 3)
    state = stage_call(
        q,
        [("own", (flat(keys0), flat(keys1)), (flat(values0), flat(values1)))]
        + beside
        + [
            ("X", (flat(x_k),), (flat(x_v),)),
            ("Y", (flat(y_k0), flat(y_k1)), (flat(y_v0), flat(y_v1))),
        ],
        None,
        lists,
        density,
    )
    *state, weights = stage_call(
        q,
        [
            ("O", (flat(o_k0), flat(o_k1)), (flat(o_v),)),
            ("W", (flat(w_k0), flat(w_k1)), (flat(w_v0), flat(w_v1))),
        ],
        state,
        lists,
        density,
        [("B", (flat(b_k),))],
    )
    weights_top = state[0]
    top, ready = stage_call(
        q, [], state, lists, density, [("GE", (flat(g_k), flat(e_k0), flat(r_k)))]
    )
    total, acc = blend_call((flat(r_v0), flat(r_v1)), ready, top, state)
    state = (top, total, acc)
    result = last_call(flat(b_v), weights, weights_top, state)
    return result.reshape(1, rows_dev, width, features)


def solution(mesh):
    in_specs = (
        P("tm", "space", None, None),
        P("tm", "space", None, None),
        P("tm", "space", None, None),
        P("tm", "space", None, None),
        P("tm", None),
    )
    out_specs = P("tm", "space", None, None)
    return jax.shard_map(body, mesh=mesh, in_specs=in_specs, out_specs=out_specs, check_vma=False)
```
